32 devices in a mesh: ha: 8 (over z, core), wa: 4 (over y, x).
Axes of the slice: x: 2, y: 2, z: 4, core: 2. Of those that a mesh axis runs over, the one named last changes fastest.
Arguments:
- latents: bfloat16 [64, 64, 64, 512], P('ha', 'wa'), may hold values from -8 to 8
- cotangent: bfloat16 [64, 64, 64, 512], P('ha', 'wa'), may hold values from -0.59765625 to 0.59765625
- w_down: bfloat16 [512, 18], replicated, may hold values from -0.25 to 0.25
- bit_bias: float32 [18], replicated, may hold values from -1.5 to 1.5
- w_up: bfloat16 [18, 512], replicated, may hold values from -1.5 to 1.5
Outputs:
- grad_latents: bfloat16 [64, 64, 64, 512], P('ha', 'wa')
- bit_entropy: float32 [64, 64, 64], P('ha', 'wa')
- marginal: float32 [18], replicated
- grad_down: float32 [512, 18], replicated
- grad_bias: float32 [18], replicated
- grad_up: float32 [18, 512], replicated
The draws below stay inside these ranges and needn't reach their ends.
All inputs are finite; a program needn't handle non-finite values.
Results may differ from the reference program's by a relative error of at most 0.005.
Values may be sent and summed in bfloat16 or wider, within the bound.
No kernel may reach another device: no remote copies, remote signals or barrier semaphores. Data moves between devices by JAX's collectives and lax.ppermute only.
A program may use at most 128 MiB of HBM per device.

```python
import jax
import jax.numpy as jnp
from jax import lax

WIDTH = 512
BITS = 18
IMAGES = 64
GRID_H = 64
GRID_W = 64


def draw_latents(key, part):
    first, second = jax.random.split(key, 2)
    height = jnp.arange(GRID_H, dtype=jnp.float32) / max(GRID_H - 1, 1)
    direction = jax.random.normal(second, (WIDTH,), jnp.float32)
    noise = jax.random.normal(first, (GRID_H, GRID_W, IMAGES, WIDTH), jnp.float32)
    field = noise + 1.2 * height[:, None, None, None] * direction
    return jnp.clip(field, -8.0, 8.0).astype(jnp.bfloat16)


def steps_of(key, shape, cuts, smallest, largest):
    level, own = 1.0, jax.random.fold_in(key, 6)
    for position, blocks in cuts:
        draws = jnp.exp(jax.random.uniform(jax.random.fold_in(own, position), (blocks,), jnp.float32, smallest / len(cuts), largest / len(cuts)))
        level = level * jnp.repeat(draws, shape[position] // blocks).reshape([-1 if axis == position else 1 for axis in range(len(shape))])
    return level


def normal_values(key, dims, scale, reach, shards=(), kind=jnp.bfloat16):
    array = jax.random.normal(key, dims, jnp.float32) * scale
    if len(shards) > 0:
        array = steps_of(key, dims, shards, -0.22, 0.18) * array
    return jnp.clip(array, min=-reach, max=reach).astype(kind)


def setup_inputs(seed: int = 0) -> dict:
    keys = jax.random.split(jax.random.key(seed), 6)
    return {
        "latents": draw_latents(jax.random.fold_in(keys[5], 71), 0),
        "cotangent": normal_values(keys[1], (GRID_H, GRID_W, IMAGES, WIDTH), 0.1, 0.59765625, ((0, 8), (1, 4))),
        "w_down": normal_values(keys[2], (WIDTH, BITS), WIDTH ** -0.5, 0.25),
        "bit_bias": jnp.clip(jax.random.uniform(keys[3], (BITS,), jnp.float32, -1.5, 1.5), -1.5, 1.5),
        "w_up": normal_values(keys[4], (BITS, WIDTH), BITS ** -0.5, 1.5),
    }


local_weight = 4.0
margin_weight = 4.0


def window(field):
    total = jnp.zeros_like(field)
    for first in (-1, 0, 1):
        for second in (-1, 0, 1):
            total = total + jnp.roll(field, (first, second), axis=(0, 1))
    return total / 9.0


def binary(values):
    return -values * jnp.log(values) - (1.0 - values) * jnp.log1p(-values)


def reference(latents, cotangent, w_down, bit_bias, w_up):
    flattened = latents.reshape(-1, WIDTH)
    outward = cotangent.reshape(-1, WIDTH)
    count = GRID_H * GRID_W * IMAGES
    logits = jnp.dot(flattened, w_down, preferred_element_type=jnp.float32) + bit_bias
    squash = jax.nn.sigmoid(logits)
    prob = 0.01 + 0.98 * squash
    pooled = window(prob.reshape(GRID_H, GRID_W, IMAGES, BITS))
    bit_entropy = jnp.sum(binary(pooled), axis=-1)
    marginal = jnp.mean(prob, axis=0)
    code = (2.0 * squash - 1.0).astype(jnp.bfloat16)
    code_grad = jnp.dot(outward, w_up.T, preferred_element_type=jnp.float32)
    slope = local_weight * jnp.log((1.0 - pooled) / pooled)
    spread = window(slope).reshape(-1, BITS)
    drift = margin_weight * jnp.log((1.0 - marginal) / marginal)
    steepness = squash * (1.0 - squash)
    base = ((2.0 * code_grad + 0.98 * spread) * steepness).astype(jnp.bfloat16)
    stacked = jnp.concatenate([base, steepness.astype(jnp.bfloat16)], axis=1)
    latent_sum = lax.dot_general(flattened, stacked, (((0,), (0,)), ((), ())), preferred_element_type=jnp.float32) / count
    column_sum = jnp.sum(stacked.astype(jnp.float32), axis=0) / count
    grad_down = latent_sum[:, :BITS] - 0.98 * drift * latent_sum[:, BITS:]
    grad_bias = column_sum[:BITS] - 0.98 * drift * column_sum[BITS:]
    grad_up = lax.dot_general(code, outward, (((0,), (0,)), ((), ())), preferred_element_type=jnp.float32) / count
    logit_grad = ((2.0 * code_grad + 0.98 * (spread - drift)) * steepness).astype(jnp.bfloat16)
    grad_latents = jnp.dot(logit_grad, w_down.T, preferred_element_type=jnp.float32).astype(jnp.bfloat16)
    grad_latents = grad_latents.reshape(latents.shape)
    return grad_latents, bit_entropy, marginal, grad_down, grad_bias, grad_up
```

```python
import functools

import jax
import jax.numpy as jnp
from jax import lax
from jax.experimental import pallas as pl
from jax.experimental.pallas import tpu as pltpu
from jax.sharding import PartitionSpec as P

local_weight = 4.0
margin_weight = 4.0
BF, F32 = jnp.bfloat16, jnp.float32


def params(mib, n=1):
    return pltpu.CompilerParams(dimension_semantics=("arbitrary",) * n, vmem_limit_bytes=mib * 2**20)


def dot(a, b, dims):
    return lax.dot_general(a, b, (dims, ((), ())), preferred_element_type=F32)


def to_column(row, n):
    eye = lax.broadcasted_iota(jnp.int32, (n, n), 0) == lax.broadcasted_iota(jnp.int32, (n, n), 1)
    return jnp.sum(jnp.where(eye, row, 0.0), axis=1, keepdims=True)


def to_row(column, n):
    eye = lax.broadcasted_iota(jnp.int32, (n, n), 0) == lax.broadcasted_iota(jnp.int32, (n, n), 1)
    return jnp.sum(jnp.where(eye, column, 0.0), axis=0, keepdims=True)


def even(axis):
    return lax.rem(lax.axis_index(axis), 2) == 0


def prob_of(squash):
    return 0.01 + 0.98 * squash


def encode_kernel(x_ref, w_ref, bias_ref, sq_ref, wt_ref, ea_ref, eb_ref, ra_ref, rb_ref, mass_ref, bias_col, mass_acc):
    r, rows = pl.program_id(0), pl.num_programs(0)
    bits = w_ref.shape[1]
    lanes = sq_ref.shape[2]
    images = x_ref.shape[2]
    edge = 2 * images

    @pl.when(r == 0)
    def _():
        wt_ref[...] = w_ref[...].astype(F32).T.astype(BF)
        bias_col[...] = jnp.broadcast_to(to_column(bias_ref[...], bits), bias_col.shape)
        mass_acc[...] = jnp.zeros_like(mass_acc)

    x = x_ref[...].reshape(lanes, x_ref.shape[3])
    logits = dot(wt_ref[...], x, ((1,), (1,))) + bias_col[:, 0:1]
    squash = jax.nn.sigmoid(logits)
    sq_ref[0] = squash
    prob = prob_of(squash)
    acc = mass_acc[...]
    for k in range(lanes // 128):
        acc += prob[:, k * 128 : (k + 1) * 128]
    mass_acc[...] = acc
    left, right = prob[:, :edge].astype(BF), prob[:, lanes - edge :].astype(BF)
    wa_even = even("wa")
    ea_ref[0, :bits] = jnp.where(wa_even, right, left)
    eb_ref[0, :bits] = jnp.where(wa_even, left, right)
    packed = prob.astype(BF)
    ha_even = even("ha")
    top, bottom = r < 2, r >= rows - 2
    slot = jnp.where(top, r, r - (rows - 2))

    @pl.when(jnp.logical_or(jnp.logical_and(top, jnp.logical_not(ha_even)), jnp.logical_and(bottom, ha_even)))
    def _():
        ra_ref[slot, :bits, edge : edge + lanes] = packed

    @pl.when(jnp.logical_or(jnp.logical_and(top, ha_even), jnp.logical_and(bottom, jnp.logical_not(ha_even))))
    def _():
        rb_ref[slot, :bits, edge : edge + lanes] = packed

    @pl.when(r == rows - 1)
    def _():
        mass_ref[...] = jnp.sum(mass_acc[...], axis=1, keepdims=True)


def encode(latents, w_down, bit_bias):
    rows, cols, images, width = latents.shape
    bits = w_down.shape[1]
    lanes, edge = cols * images, 2 * images
    padded = -(-bits // 16) * 16
    whole = lambda *shape: pl.BlockSpec(shape, lambda r: (0,) * len(shape))
    return pl.pallas_call(
        encode_kernel,
        grid=(rows,),
        in_specs=[
            pl.BlockSpec((1, cols, images, width), lambda r: (r, 0, 0, 0)),
            whole(width, bits),
            whole(1, bits),
        ],
        out_specs=[
            pl.BlockSpec((1, bits, lanes), lambda r: (r, 0, 0)),
            whole(bits, width),
            pl.BlockSpec((1, padded, edge), lambda r: (r, 0, 0)),
            pl.BlockSpec((1, padded, edge), lambda r: (r, 0, 0)),
            whole(2, padded, lanes + 2 * edge),
            whole(2, padded, lanes + 2 * edge),
            whole(bits, 1),
        ],
        out_shape=[
            jax.ShapeDtypeStruct((rows, bits, lanes), F32),
            jax.ShapeDtypeStruct((bits, width), BF),
            jax.ShapeDtypeStruct((rows, padded, edge), BF),
            jax.ShapeDtypeStruct((rows, padded, edge), BF),
            jax.ShapeDtypeStruct((2, padded, lanes + 2 * edge), BF),
            jax.ShapeDtypeStruct((2, padded, lanes + 2 * edge), BF),
            jax.ShapeDtypeStruct((bits, 1), F32),
        ],
        scratch_shapes=[pltpu.VMEM((bits, 128), F32), pltpu.VMEM((bits, 128), F32)],
        compiler_params=params(12),
        cost_estimate=pl.CostEstimate(flops=2 * rows * lanes * width * 256, bytes_accessed=latents.size * 2, transcendentals=0),
        name="encode",
    )(latents, w_down, bit_bias)


def outward_kernel(x_ref, w_ref, sq_ref, cg_ref, up_ref):
    r = pl.program_id(0)
    x = x_ref[...].reshape(sq_ref.shape[2], x_ref.shape[3])
    code = (2.0 * sq_ref[0] - 1.0).astype(BF)
    cg_ref[0] = dot(w_ref[...], x, ((1,), (1,)))
    part = dot(code, x, ((1,), (0,)))

    @pl.when(r == 0)
    def _():
        up_ref[...] = part

    @pl.when(r > 0)
    def _():
        up_ref[...] += part


def outward_part(cotangent, w_up, squash, first, rows):
    _, cols, images, width = cotangent.shape
    bits, lanes = w_up.shape[0], cols * images
    return pl.pallas_call(
        outward_kernel,
        grid=(rows,),
        in_specs=[
            pl.BlockSpec((1, cols, images, width), lambda r: (r + first, 0, 0, 0)),
            pl.BlockSpec((bits, width), lambda r: (0, 0)),
            pl.BlockSpec((1, bits, lanes), lambda r: (r + first, 0, 0)),
        ],
        out_specs=[pl.BlockSpec((1, bits, lanes), lambda r: (r, 0, 0)), pl.BlockSpec((bits, width), lambda r: (0, 0))],
        out_shape=[jax.ShapeDtypeStruct((rows, bits, lanes), F32), jax.ShapeDtypeStruct((bits, width), F32)],
        compiler_params=params(12),
        cost_estimate=pl.CostEstimate(flops=2 * rows * lanes * width * 256, bytes_accessed=rows * lanes * width * 2, transcendentals=0),
        name="outward",
    )(cotangent, w_up, squash)


def spread_kernel(
    x_ref, sq_ref, cg_ref, wa_a, wa_b, ha_a, ha_b, up_ref, mass_ref,
    g_ref, ent_ref, mine_ref, other_ref,
    pe, slope, stacked, acc, columns,
):
    r, rows = pl.program_id(0), pl.num_programs(0)
    bits, lanes = sq_ref.shape[1], sq_ref.shape[2]
    images = x_ref.shape[2]
    edge, wide = 2 * images, lanes + 2 * images

    def slope_row(e):
        t = pe[e] + pe[e + 1] + pe[e + 2]
        pooled = (t[:, :wide] + t[:, images : images + wide] + t[:, 2 * images :]) / 9.0
        lp, lq = jnp.log(pooled), jnp.log(1.0 - pooled)
        slope[e] = local_weight * (lq - lp)
        return lq + pooled * (lp - lq)

    @pl.when(r == 0)
    def _():
        stacked[...] = jnp.zeros_like(stacked)
        columns[...] = jnp.zeros_like(columns)
        acc[...] = jnp.zeros_like(acc)
        wa_even, ha_even = even("wa"), even("ha")
        for k in range(sq_ref.shape[0]):
            pe[k + 2, :, edge : edge + lanes] = prob_of(sq_ref[k])
            a, b = wa_a[k, :bits].astype(F32), wa_b[k, :bits].astype(F32)
            pe[k + 2, :, :edge] = jnp.where(wa_even, b, a)
            pe[k + 2, :, edge + lanes :] = jnp.where(wa_even, a, b)
        for k in range(2):
            a, b = ha_a[k, :bits].astype(F32), ha_b[k, :bits].astype(F32)
            pe[k] = jnp.where(ha_even, b, a)
            pe[sq_ref.shape[0] + 2 + k] = jnp.where(ha_even, a, b)
        slope_row(0)
        first = slope_row(1)
        ent_ref[pl.ds(0, 1), :] = -jnp.sum(first, axis=0, keepdims=True)[:, images : images + lanes]

    following = slope_row(r + 2)

    @pl.when(r < rows - 1)
    def _():
        ent_ref[pl.ds(r + 1, 1), :] = -jnp.sum(following, axis=0, keepdims=True)[:, images : images + lanes]

    t = slope[r] + slope[r + 1] + slope[r + 2]
    spread = (t[:, :lanes] + t[:, images : images + lanes] + t[:, 2 * images :]) / 9.0
    squash = sq_ref[r]
    steep = squash * (1.0 - squash)
    g = 2.0 * cg_ref[r] + 0.98 * spread
    g_ref[0] = g
    base, flat = (g * steep).astype(BF), steep.astype(BF)
    half = stacked.shape[0] // 2
    stacked[:bits] = base
    stacked[half : half + bits] = flat
    x = x_ref[...].reshape(lanes, x_ref.shape[3])
    values = stacked[...]
    acc[...] += dot(values, x, ((1,), (0,)))
    total = columns[...]
    for k in range(lanes // 128):
        total += values[:, k * 128 : (k + 1) * 128].astype(F32)
    columns[...] = total

    @pl.when(r == rows - 1)
    def _():
        core = even("ha")
        width = acc.shape[1]
        sums = jnp.sum(columns[...], axis=1, keepdims=True)
        rows_of = (to_row(sums[:bits], bits), to_row(sums[half : half + bits], bits), to_row(mass_ref[...], bits))
        low, high = slice(0, width // 2), slice(width // 2, width)
        pieces = (
            (0, acc[:bits]),
            (bits, acc[half : half + bits]),
            (2 * bits, up_ref[...]),
        )
        for ref, flip in ((mine_ref, False), (other_ref, True)):
            ref[3 * bits :, :] = jnp.zeros((ref.shape[0] - 3 * bits, ref.shape[1]), F32)
            take_low = jnp.logical_xor(core, flip)
            for at, piece in pieces:
                ref[at : at + bits] = jnp.where(take_low, piece[:, low], piece[:, high])
            ref[3 * bits : 3 * bits + 1, :bits] = rows_of[0]
            ref[3 * bits : 3 * bits + 1, 128 : 128 + bits] = rows_of[1]
            ref[3 * bits + 1 : 3 * bits + 2, :bits] = rows_of[2]


def spread_part(latents, squash, cg, halos, up, mass):
    rows, cols, images, width = latents.shape
    bits, lanes = squash.shape[1], squash.shape[2]
    padded = -(-bits // 16) * 16
    sums = -(-(3 * bits + 2) // 8) * 8
    whole = lambda a: pl.BlockSpec(a.shape, lambda r, n=len(a.shape): (0,) * n)
    full = [squash, cg, *halos, up, mass]
    return pl.pallas_call(
        spread_kernel,
        grid=(rows,),
        in_specs=[pl.BlockSpec((1, cols, images, width), lambda r: (r, 0, 0, 0)), *map(whole, full)],
        out_specs=[
            pl.BlockSpec((1, bits, lanes), lambda r: (r, 0, 0)),
            pl.BlockSpec((rows, lanes), lambda r: (0, 0)),
            pl.BlockSpec((sums, width // 2), lambda r: (0, 0)),
            pl.BlockSpec((sums, width // 2), lambda r: (0, 0)),
        ],
        out_shape=[
            jax.ShapeDtypeStruct((rows, bits, lanes), F32),
            jax.ShapeDtypeStruct((rows, lanes), F32),
            jax.ShapeDtypeStruct((sums, width // 2), F32),
            jax.ShapeDtypeStruct((sums, width // 2), F32),
        ],
        scratch_shapes=[
            pltpu.VMEM((rows + 4, bits, lanes + 4 * images), F32),
            pltpu.VMEM((rows + 2, bits, lanes + 2 * images), F32),
            pltpu.VMEM((2 * padded, lanes), BF),
            pltpu.VMEM((2 * padded, width), F32),
            pltpu.VMEM((2 * padded, 128), F32),
        ],
        compiler_params=params(20),
        cost_estimate=pl.CostEstimate(flops=2 * rows * lanes * width * 256, bytes_accessed=latents.size * 2, transcendentals=0),
        name="spread",
    )(latents, *full)


def drift_of(mass_row, count, bits):
    marginal = to_column(mass_row, bits) / count
    return margin_weight * jnp.log((1.0 - marginal) / marginal)


def back_kernel(count, g_ref, sq_ref, sums_ref, wt_ref, out_ref):
    bits = g_ref.shape[1]
    drift = drift_of(sums_ref[3 * bits + 1 : 3 * bits + 2, :bits], count, bits)
    squash = sq_ref[0]
    grad = ((g_ref[0] - 0.98 * drift) * (squash * (1.0 - squash))).astype(BF)
    out = dot(grad, wt_ref[...], ((0,), (0,)))
    out_ref[...] = out.astype(BF).reshape(out_ref.shape)


def back(shape, g, squash, sums, wt, count):
    rows, cols, images, width = shape
    bits, lanes = squash.shape[1], squash.shape[2]
    row = pl.BlockSpec((1, bits, lanes), lambda r: (r, 0, 0))
    return pl.pallas_call(
        functools.partial(back_kernel, count),
        grid=(rows,),
        in_specs=[row, row, pl.BlockSpec(sums.shape, lambda r: (0, 0)), pl.BlockSpec(wt.shape, lambda r: (0, 0))],
        out_specs=pl.BlockSpec((1, cols, images, width), lambda r: (r, 0, 0, 0)),
        out_shape=jax.ShapeDtypeStruct(shape, BF),
        compiler_params=params(16),
        cost_estimate=pl.CostEstimate(flops=2 * rows * lanes * width * 256, bytes_accessed=rows * lanes * width * 2, transcendentals=0),
        name="back",
    )(g, squash, sums, wt)


def finish_kernel(count, mine_ref, other_ref, marginal_ref, down_ref, bias_ref, up_ref):
    bits = marginal_ref.shape[1]
    core = even("ha")
    a, b = mine_ref[...], other_ref[...]
    sums = jnp.concatenate([jnp.where(core, a, b), jnp.where(core, b, a)], axis=1)
    mass = mine_ref[3 * bits + 1 : 3 * bits + 2, :bits]
    marginal = mass / count
    marginal_ref[...] = marginal
    drift_row = margin_weight * jnp.log((1.0 - marginal) / marginal)
    drift = to_column(drift_row, bits)
    down = (sums[:bits] - 0.98 * drift * sums[bits : 2 * bits]) / count
    down_ref[...] = down.T
    bias_ref[...] = (mine_ref[3 * bits : 3 * bits + 1, :bits] - 0.98 * drift_row * mine_ref[3 * bits : 3 * bits + 1, 128 : 128 + bits]) / count
    up_ref[...] = sums[2 * bits : 3 * bits] / count


def finish(mine, other, bits, count):
    width = 2 * mine.shape[1]
    return pl.pallas_call(
        functools.partial(finish_kernel, count),
        out_shape=[
            jax.ShapeDtypeStruct((1, bits), F32),
            jax.ShapeDtypeStruct((width, bits), F32),
            jax.ShapeDtypeStruct((1, bits), F32),
            jax.ShapeDtypeStruct((bits, width), F32),
        ],
        compiler_params=pltpu.CompilerParams(vmem_limit_bytes=8 * 2**20),
        name="finish",
    )(mine, other)


def swap(x, axis, mask):
    return lax.ppermute(x, axis, [(i, i ^ mask) for i in range(lax.axis_size(axis))])


def swap_outer(x, axis):
    count = lax.axis_size(axis)
    return lax.ppermute(x, axis, [(i, (((i + 1) ^ 1) - 1) % count) for i in range(count)])


def summed(x, axis, start):
    count, stride = lax.axis_size(axis), start
    while stride < count:
        radix = 4 if stride * 4 <= count else 2
        parts = [swap(x, axis, d * stride) for d in range(1, radix)]
        for part in parts:
            x = x + part
        stride *= radix
    return x


def local(latents, cotangent, w_down, bit_bias, w_up):
    rows, cols, images, width = latents.shape
    bits = w_down.shape[1]
    count = rows * cols * images * lax.axis_size("ha") * lax.axis_size("wa")
    edge = 2 * images
    squash, wt, ea, eb, ra, rb, mass = encode(latents, w_down, bit_bias.reshape(1, bits))
    wa_a, wa_b = swap(ea, "wa", 1), swap_outer(eb, "wa")
    cg0, up0 = outward_part(cotangent, w_up, squash, 0, rows)
    wa_even, ha_even = even("wa"), even("ha")
    left, right = jnp.where(wa_even, wa_b, wa_a), jnp.where(wa_even, wa_a, wa_b)

    def sides(payload, at_bottom):
        head, tail = (jnp.where(at_bottom, side[rows - 2 :], side[:2]) for side in (left, right))
        payload = lax.dynamic_update_slice(payload, head, (0, 0, 0))
        return lax.dynamic_update_slice(payload, tail, (0, 0, edge + cols * images))

    ha_a = swap(sides(ra, ha_even), "ha", 1)
    ha_b = swap_outer(sides(rb, jnp.logical_not(ha_even)), "ha")
    g, entropy, mine, other = spread_part(latents, squash, cg0, (wa_a, wa_b, ha_a, ha_b), up0, mass)
    sums = mine + swap(other, "ha", 1)
    sums = summed(sums, "wa", 1)
    sums = summed(sums, "ha", 2)
    grad_latents = back(latents.shape, g, squash, sums, wt, count)
    partner = swap(sums, "ha", 1)
    marginal, grad_down, grad_bias, grad_up = finish(sums, partner, bits, count)
    return (
        grad_latents,
        entropy.reshape(rows, cols, images),
        marginal.reshape(bits),
        grad_down,
        grad_bias.reshape(bits),
        grad_up,
    )


def solution(mesh):
    placed = (P("ha", "wa", None, None), P("ha", "wa", None, None), P(), P(), P())
    return jax.shard_map(
        local,
        mesh=mesh,
        in_specs=placed,
        out_specs=(P("ha", "wa", None, None), P("ha", "wa", None), P(), P(), P(), P()),
        check_vma=False,
    )
```

```python
import functools

import jax
import jax.numpy as jnp
from jax import lax
from jax.experimental import pallas as pl
from jax.experimental.pallas import tpu as pltpu
from jax.sharding import PartitionSpec as P

local_weight = 4.0
margin_weight = 4.0
BF, F32 = jnp.bfloat16, jnp.float32


VMEM = pl.BlockSpec(memory_space=pltpu.VMEM)
HBM = pl.BlockSpec(memory_space=pltpu.HBM)


def params(mib):
    return pltpu.CompilerParams(vmem_limit_bytes=mib * 2**20)


def cost(flops, bytes_accessed):
    return pl.CostEstimate(flops=flops, bytes_accessed=bytes_accessed, transcendentals=0)


def dot(a, b, dims):
    return lax.dot_general(a, b, (dims, ((), ())), preferred_element_type=F32)


def to_column(row, n):
    eye = lax.broadcasted_iota(jnp.int32, (n, n), 0) == lax.broadcasted_iota(jnp.int32, (n, n), 1)
    return jnp.sum(jnp.where(eye, row, 0.0), axis=1, keepdims=True)


def to_row(column, n):
    eye = lax.broadcasted_iota(jnp.int32, (n, n), 0) == lax.broadcasted_iota(jnp.int32, (n, n), 1)
    return jnp.sum(jnp.where(eye, column, 0.0), axis=0, keepdims=True)


def even(axis):
    return lax.rem(lax.axis_index(axis), 2) == 0


def prob_of(squash):
    return 0.01 + 0.98 * squash


def encode_kernel(x_hbm, wt_ref, bias_ref, x_ref, sq_ref, ea_ref, eb_ref, ra_ref, rb_ref, mass_ref, sem):
    rows, bits, lanes = sq_ref.shape
    images, width = x_hbm.shape[2:]
    edge = 2 * images
    copies = [pltpu.make_async_copy(x_hbm.at[r], x_ref.at[r], sem.at[r]) for r in range(rows)]
    for copy in copies:
        copy.start()
    wt = wt_ref[...]
    bias = to_column(bias_ref[...], bits)
    wa_even, ha_even = even("wa"), even("ha")
    mass = jnp.zeros((bits, 128), F32)
    keep = {}
    for r, copy in enumerate(copies):
        copy.wait()
        logits = dot(wt, x_ref[r].reshape(lanes, width), ((1,), (1,))) + bias
        squash = jax.nn.sigmoid(logits)
        sq_ref[r] = squash
        prob = prob_of(squash)
        for k in range(lanes // 128):
            mass += prob[:, k * 128 : (k + 1) * 128]
        left, right = logits[:, :edge].astype(BF), logits[:, lanes - edge :].astype(BF)
        ea_ref[r, :bits] = jnp.where(wa_even, right, left)
        eb_ref[r, :bits] = jnp.where(wa_even, left, right)
        if r < 2:
            keep[r] = logits.astype(BF)
        if r >= rows - 2:
            k = r - (rows - 2)
            top, bottom = keep[k], logits.astype(BF)
            ra_ref[k, :bits, edge : edge + lanes] = jnp.where(ha_even, bottom, top)
            rb_ref[k, :bits, edge : edge + lanes] = jnp.where(ha_even, top, bottom)
    mass_ref[...] = jnp.sum(mass, axis=1, keepdims=True)


def encode(latents, wt, bit_bias):
    rows, cols, images, width = latents.shape
    bits = wt.shape[0]
    lanes, edge = cols * images, 2 * images
    padded = -(-bits // 16) * 16
    shape = jax.ShapeDtypeStruct
    return pl.pallas_call(
        encode_kernel,
        in_specs=[HBM, VMEM, VMEM],
        out_specs=[VMEM] * 7,
        out_shape=[
            pltpu.VMEM(latents.shape, BF),
            shape((rows, bits, lanes), F32),
            shape((rows, padded, edge), BF),
            shape((rows, padded, edge), BF),
            shape((2, padded, lanes + 2 * edge), BF),
            shape((2, padded, lanes + 2 * edge), BF),
            shape((bits, 1), F32),
        ],
        scratch_shapes=[pltpu.SemaphoreType.DMA((rows,))],
        compiler_params=params(8),
        cost_estimate=cost(2 * rows * lanes * width * 256, latents.size * 2),
        name="encode",
    )(latents, wt, bit_bias)


def pack_kernel(wa_a, wa_b, ra_ref, rb_ref, after, ra_out, rb_out):
    rows, _, edge = wa_a.shape
    lanes = ra_ref.shape[2] - 2 * edge
    wa_even, ha_even = even("wa"), even("ha")
    for k in range(2):
        ends = [(wa_a[r], wa_b[r]) for r in (k, rows - 2 + k)]
        (top_l, top_r), (bot_l, bot_r) = [(jnp.where(wa_even, b, a), jnp.where(wa_even, a, b)) for a, b in ends]
        for out, own, low in ((ra_out, ra_ref, ha_even), (rb_out, rb_ref, jnp.logical_not(ha_even))):
            out[k, :, edge : edge + lanes] = own[k, :, edge : edge + lanes]
            out[k, :, :edge] = jnp.where(low, bot_l, top_l)
            out[k, :, edge + lanes :] = jnp.where(low, bot_r, top_r)


def pack(wa_a, wa_b, ra, rb, after):
    return pl.pallas_call(
        pack_kernel,
        in_specs=[VMEM] * 4 + [pl.BlockSpec(memory_space=pl.ANY)],
        out_specs=[VMEM] * 2,
        out_shape=[jax.ShapeDtypeStruct(a.shape, a.dtype) for a in (ra, rb)],
        compiler_params=params(2),
        cost_estimate=cost(0, 2**18),
        name="pack",
    )(wa_a, wa_b, ra, rb, after)


def outward_kernel(x_hbm, w_ref, sq_ref, cg_ref, up_ref, x_ref, sem):
    rows, bits, lanes = sq_ref.shape
    width = x_hbm.shape[3]
    copies = [pltpu.make_async_copy(x_hbm.at[r], x_ref.at[r], sem.at[r]) for r in range(rows)]
    for copy in copies:
        copy.start()
    w = w_ref[...]
    total = jnp.zeros((bits, width), F32)
    for r, copy in enumerate(copies):
        copy.wait()
        x = x_ref[r].reshape(lanes, width)
        code = (2.0 * sq_ref[r] - 1.0).astype(BF)
        cg_ref[r] = dot(w, x, ((1,), (1,)))
        total += dot(code, x, ((1,), (0,)))
    up_ref[...] = total


def outward(cotangent, w_up, squash):
    rows, cols, images, width = cotangent.shape
    bits, lanes = w_up.shape[0], cols * images
    return pl.pallas_call(
        outward_kernel,
        in_specs=[HBM, VMEM, VMEM],
        out_specs=[VMEM] * 2,
        out_shape=[jax.ShapeDtypeStruct((rows, bits, lanes), F32), jax.ShapeDtypeStruct((bits, width), F32)],
        scratch_shapes=[pltpu.VMEM(cotangent.shape, BF), pltpu.SemaphoreType.DMA((rows,))],
        compiler_params=params(12),
        cost_estimate=cost(4 * rows * lanes * width * 256, cotangent.size * 2),
        name="outward",
    )(cotangent, w_up, squash)


def fill_row(pe, k, squash, left, right):
    lanes, edge = squash.shape[1], left.shape[1]
    pe[k, :, edge : edge + lanes] = prob_of(squash)
    pe[k, :, :edge] = prob_of(jax.nn.sigmoid(left.astype(F32)))
    pe[k, :, edge + lanes :] = prob_of(jax.nn.sigmoid(right.astype(F32)))


def slopes(pe, k, images):
    wide = pe.shape[2] - 2 * images
    t = pe[k] + pe[k + 1] + pe[k + 2]
    pooled = (t[:, :wide] + t[:, images : images + wide] + t[:, 2 * images :]) / 9.0
    lp, lq = jnp.log(pooled), jnp.log(1.0 - pooled)
    entropy = jnp.sum(pooled * (lq - lp) - lq, axis=0, keepdims=True)
    return local_weight * (lq - lp), entropy[:, images : wide - images]


def gradients(slope, squash, cg, g_ref, stacked, images):
    bits, lanes = squash.shape
    half = stacked.shape[0] // 2
    t = slope[0] + slope[1] + slope[2]
    spread = (t[:, :lanes] + t[:, images : images + lanes] + t[:, 2 * images :]) / 9.0
    steep = squash * (1.0 - squash)
    g = 2.0 * cg + 0.98 * spread
    g_ref[...] = g
    stacked[:bits] = (g * steep).astype(BF)
    stacked[half : half + bits] = steep.astype(BF)
    values = stacked[...]
    columns = values[:, :128].astype(F32)
    for k in range(1, lanes // 128):
        columns += values[:, k * 128 : (k + 1) * 128].astype(F32)
    return values, columns


def inner_kernel(x_ref, sq_ref, cg_ref, wa_a, wa_b, g_ref, slope_ref, ent_ref, acc_ref, columns_ref, pe, stacked):
    rows, bits, lanes = sq_ref.shape
    images, width = x_ref.shape[2:]
    wa_even = even("wa")
    stacked[...] = jnp.zeros_like(stacked)
    for k in range(rows):
        a, b = wa_a[k, :bits], wa_b[k, :bits]
        fill_row(pe, k, sq_ref[k], jnp.where(wa_even, b, a), jnp.where(wa_even, a, b))
    acc = jnp.zeros(acc_ref.shape, F32)
    columns = jnp.zeros(columns_ref.shape, F32)
    for r in range(1, rows - 1):
        slope_ref[r - 1], ent_ref[r : r + 1] = slopes(pe, r - 1, images)
        done = r - 1
        if done >= 2:
            values, sums = gradients(
                [slope_ref[done - 2], slope_ref[done - 1], slope_ref[done]], sq_ref[done], cg_ref[done], g_ref.at[done - 2], stacked.at[done % 2], images
            )
            acc += dot(values, x_ref[done].reshape(lanes, width), ((1,), (0,)))
            columns += sums
    ent_ref[0:1] = jnp.zeros((1, lanes), F32)
    ent_ref[rows - 1 : rows] = jnp.zeros((1, lanes), F32)
    acc_ref[...] = acc
    columns_ref[...] = columns


def inner(x, squash, cg, wa_a, wa_b):
    images, width = x.shape[2:]
    rows, bits, lanes = squash.shape
    padded = -(-bits // 16) * 16
    shape = lambda *dims: jax.ShapeDtypeStruct(dims, F32)
    return pl.pallas_call(
        inner_kernel,
        in_specs=[VMEM] * 5,
        out_specs=[VMEM] * 5,
        out_shape=[
            shape(rows - 4, bits, lanes),
            shape(rows - 2, bits, lanes + 2 * images),
            shape(rows, lanes),
            shape(2 * padded, width),
            shape(2 * padded, 128),
        ],
        scratch_shapes=[pltpu.VMEM((rows, bits, lanes + 4 * images), F32), pltpu.VMEM((2, 2 * padded, lanes), BF)],
        compiler_params=params(8),
        cost_estimate=cost(2 * rows // 2 * lanes * width * 256, 2**20),
        name="inner",
    )(x, squash, cg, wa_a, wa_b)


def outer_kernel(
    x_ref, sq_ref, cg_ref, wa_a, wa_b, ha_a, ha_b, slope_ref, ent_in, acc_ref, columns_ref, up_ref, mass_ref,
    g_ref, ent_ref, mine_ref, other_ref,
    pe, stacked,
):
    rows, bits, lanes = sq_ref.shape
    images, width = x_ref.shape[2:]
    half = stacked.shape[1] // 2
    wa_even, ha_even = even("wa"), even("ha")
    stacked[...] = jnp.zeros_like(stacked)
    for k in range(2):
        a, b = ha_a[k, :bits], ha_b[k, :bits]
        pe[k] = prob_of(jax.nn.sigmoid(jnp.where(ha_even, b, a).astype(F32)))
        pe[6 + k] = prob_of(jax.nn.sigmoid(jnp.where(ha_even, a, b).astype(F32)))
    for k, r in ((2, 0), (3, 1), (4, rows - 2), (5, rows - 1)):
        a, b = wa_a[r, :bits], wa_b[r, :bits]
        fill_row(pe, k, sq_ref[r], jnp.where(wa_even, b, a), jnp.where(wa_even, a, b))
    ent_ref[...] = ent_in[...]
    before, _ = slopes(pe, 0, images)
    first, ent_ref[0:1] = slopes(pe, 1, images)
    last, ent_ref[rows - 1 : rows] = slopes(pe, 4, images)
    after, _ = slopes(pe, 5, images)
    plans = (
        (0, (before, first, slope_ref[0])),
        (1, (first, slope_ref[0], slope_ref[1])),
        (rows - 2, (slope_ref[rows - 4], slope_ref[rows - 3], last)),
        (rows - 1, (slope_ref[rows - 3], last, after)),
    )
    acc, columns = acc_ref[...], columns_ref[...]
    for k, (r, around) in enumerate(plans):
        values, sums = gradients(around, sq_ref[r], cg_ref[r], g_ref.at[k], stacked.at[k % 2], images)
        acc += dot(values, x_ref[r].reshape(lanes, width), ((1,), (0,)))
        columns += sums
    total = jnp.sum(columns, axis=1, keepdims=True)
    rows_of = (to_row(total[:bits], bits), to_row(total[half : half + bits], bits), to_row(mass_ref[...], bits))
    low, high = slice(0, width // 2), slice(width // 2, width)
    pieces = ((0, acc[:bits]), (bits, acc[half : half + bits]), (2 * bits, up_ref[...]))
    for ref, flip in ((mine_ref, False), (other_ref, True)):
        ref[3 * bits :, :] = jnp.zeros((ref.shape[0] - 3 * bits, ref.shape[1]), F32)
        take_low = jnp.logical_xor(ha_even, flip)
        for at, piece in pieces:
            ref[at : at + bits] = jnp.where(take_low, piece[:, low], piece[:, high])
        ref[3 * bits : 3 * bits + 1, :bits] = rows_of[0]
        ref[3 * bits : 3 * bits + 1, 128 : 128 + bits] = rows_of[1]
        ref[3 * bits + 1 : 3 * bits + 2, :bits] = rows_of[2]


def outer(x, squash, cg, halos, inside, up, mass):
    images, width = x.shape[2:]
    rows, bits, lanes = squash.shape
    padded = -(-bits // 16) * 16
    sums = -(-(3 * bits + 2) // 8) * 8
    shape = lambda *dims: jax.ShapeDtypeStruct(dims, F32)
    return pl.pallas_call(
        outer_kernel,
        in_specs=[VMEM] * 13,
        out_specs=[VMEM] * 4,
        out_shape=[shape(4, bits, lanes), shape(rows, lanes), shape(sums, width // 2), shape(sums, width // 2)],
        scratch_shapes=[pltpu.VMEM((8, bits, lanes + 4 * images), F32), pltpu.VMEM((2, 2 * padded, lanes), BF)],
        compiler_params=params(8),
        cost_estimate=cost(2 * 4 * lanes * width * 256, 2**20),
        name="outer",
    )(x, squash, cg, *halos, *inside, up, mass)


def drift_of(mass_row, count, bits):
    marginal = to_column(mass_row, bits) / count
    return margin_weight * jnp.log((1.0 - marginal) / marginal)


def back_kernel(count, gi_ref, go_ref, sq_ref, sums_ref, wt_ref, out_hbm, out_ref, sem):
    rows, bits, lanes = sq_ref.shape
    drift = 0.98 * drift_of(sums_ref[3 * bits + 1 : 3 * bits + 2, :bits], count, bits)
    wt = wt_ref[...]
    copies = [pltpu.make_async_copy(out_ref.at[r], out_hbm.at[r], sem.at[r]) for r in range(rows)]
    for r, copy in enumerate(copies):
        squash = sq_ref[r]
        g = gi_ref[r - 2] if 2 <= r < rows - 2 else go_ref[r if r < 2 else r - (rows - 4)]
        grad = ((g - drift) * (squash * (1.0 - squash))).astype(BF)
        out_ref[r] = dot(grad, wt, ((0,), (0,))).astype(BF).reshape(out_ref.shape[1:])
        copy.start()
    for copy in copies:
        copy.wait()


def back(shape, g_inner, g_outer, squash, sums, wt, count):
    rows, bits, lanes = squash.shape
    width = shape[3]
    return pl.pallas_call(
        functools.partial(back_kernel, count),
        in_specs=[VMEM] * 5,
        out_specs=HBM,
        out_shape=jax.ShapeDtypeStruct(shape, BF),
        scratch_shapes=[pltpu.VMEM(shape, BF), pltpu.SemaphoreType.DMA((rows,))],
        compiler_params=params(16),
        cost_estimate=cost(2 * rows * lanes * width * 256, rows * lanes * width * 2),
        name="back",
    )(g_inner, g_outer, squash, sums, wt)


def finish_kernel(count, mine_ref, other_ref, marginal_ref, down_ref, bias_ref, up_ref):
    bits = marginal_ref.shape[1]
    core = even("ha")
    a, b = mine_ref[...], other_ref[...]
    sums = jnp.concatenate([jnp.where(core, a, b), jnp.where(core, b, a)], axis=1)
    mass = mine_ref[3 * bits + 1 : 3 * bits + 2, :bits]
    marginal = mass / count
    marginal_ref[...] = marginal
    drift_row = margin_weight * jnp.log((1.0 - marginal) / marginal)
    drift = to_column(drift_row, bits)
    down = (sums[:bits] - 0.98 * drift * sums[bits : 2 * bits]) / count
    down_ref[...] = down
    bias_ref[...] = (mine_ref[3 * bits : 3 * bits + 1, :bits] - 0.98 * drift_row * mine_ref[3 * bits : 3 * bits + 1, 128 : 128 + bits]) / count
    up_ref[...] = sums[2 * bits : 3 * bits] / count


def finish(mine, other, bits, count):
    width = 2 * mine.shape[1]
    return pl.pallas_call(
        functools.partial(finish_kernel, count),
        out_shape=[
            jax.ShapeDtypeStruct((1, bits), F32),
            jax.ShapeDtypeStruct((bits, width), F32),
            jax.ShapeDtypeStruct((1, bits), F32),
            jax.ShapeDtypeStruct((bits, width), F32),
        ],
        compiler_params=pltpu.CompilerParams(vmem_limit_bytes=8 * 2**20),
        name="finish",
    )(mine, other)


def swap(x, axis, mask):
    return lax.ppermute(x, axis, [(i, i ^ mask) for i in range(lax.axis_size(axis))])


def swap_outer(x, axis):
    count = lax.axis_size(axis)
    return lax.ppermute(x, axis, [(i, (((i + 1) ^ 1) - 1) % count) for i in range(count)])


def summed(x, axis, start):
    count, stride = lax.axis_size(axis), start
    while stride < count:
        radix = 4 if stride * 4 <= count else 2
        parts = [swap(x, axis, d * stride) for d in range(1, radix)]
        for part in parts:
            x = x + part
        stride *= radix
    return x


def local(latents, cotangent, w_down, bit_bias, w_up):
    rows, cols, images, width = latents.shape
    bits = w_down.shape[1]
    count = rows * cols * images * lax.axis_size("ha") * lax.axis_size("wa")
    edge = 2 * images
    wt = w_down.T
    latents, cotangent = (pltpu.with_memory_space_constraint(a, pltpu.HBM) for a in (latents, cotangent))
    x, squash, ea, eb, ra, rb, mass = encode(latents, wt, bit_bias.reshape(1, bits))
    x = pltpu.with_memory_space_constraint(x, pltpu.VMEM)
    wa_a, wa_b = swap(ea, "wa", 1), swap_outer(eb, "wa")
    cg, up = outward(cotangent, w_up, squash)
    ra, rb = pack(wa_a, wa_b, ra, rb, up)
    ha_a, ha_b = swap(ra, "ha", 1), swap_outer(rb, "ha")
    g_inner, *inside = inner(x, squash, cg, wa_a, wa_b)
    g_outer, entropy, mine, other = outer(x, squash, cg, (wa_a, wa_b, ha_a, ha_b), inside, up, mass)
    sums = mine + swap(other, "ha", 1)
    sums = summed(sums, "wa", 1)
    sums = summed(sums, "ha", 2)
    grad_latents = back(latents.shape, g_inner, g_outer, squash, sums, wt, count)
    partner = swap(sums, "ha", 1)
    marginal, grad_down, grad_bias, grad_up = finish(sums, partner, bits, count)
    return (
        grad_latents,
        entropy.reshape(rows, cols, images),
        marginal.reshape(bits),
        grad_down.T,
        grad_bias.reshape(bits),
        grad_up,
    )


def solution(mesh):
    placed = (P("ha", "wa", None, None), P("ha", "wa", None, None), P(), P(), P())
    return jax.shard_map(
        local,
        mesh=mesh,
        in_specs=placed,
        out_specs=(P("ha", "wa", None, None), P("ha", "wa", None), P(), P(), P(), P()),
        check_vma=False,
    )
```

```python
import functools

import jax
import jax.numpy as jnp
from jax import lax
from jax.experimental import pallas as pl
from jax.experimental.pallas import tpu as pltpu
from jax.sharding import PartitionSpec as P

local_weight = 4.0
margin_weight = 4.0
BF, F32 = jnp.bfloat16, jnp.float32


VMEM = pl.BlockSpec(memory_space=pltpu.VMEM)
HBM = pl.BlockSpec(memory_space=pltpu.HBM)


def params(mib):
    return pltpu.CompilerParams(vmem_limit_bytes=mib * 2**20)


def cost(flops, bytes_accessed):
    return pl.CostEstimate(flops=flops, bytes_accessed=bytes_accessed, transcendentals=0)


def dot(a, b, dims):
    return lax.dot_general(a, b, (dims, ((), ())), preferred_element_type=F32)


def to_column(row, n):
    eye = lax.broadcasted_iota(jnp.int32, (n, n), 0) == lax.broadcasted_iota(jnp.int32, (n, n), 1)
    return jnp.sum(jnp.where(eye, row, 0.0), axis=1, keepdims=True)


def to_row(column, n):
    eye = lax.broadcasted_iota(jnp.int32, (n, n), 0) == lax.broadcasted_iota(jnp.int32, (n, n), 1)
    return jnp.sum(jnp.where(eye, column, 0.0), axis=0, keepdims=True)


def even(axis):
    return lax.rem(lax.axis_index(axis), 2) == 0


def prob_of(squash):
    return 0.01 + 0.98 * squash


def encode_kernel(x_hbm, wt_hbm, bias_hbm, x_ref, sq_ref, ea_ref, eb_ref, ra_ref, rb_ref, mass_ref, wt_ref, bias_ref, sem):
    rows, bits, lanes = sq_ref.shape
    images, width = x_hbm.shape[2:]
    edge = 2 * images
    copies = [pltpu.make_async_copy(x_hbm.at[r], x_ref.at[r], sem.at[r]) for r in range(rows)]
    small = [
        pltpu.make_async_copy(wt_hbm, wt_ref, sem.at[rows]),
        pltpu.make_async_copy(bias_hbm, bias_ref, sem.at[rows + 1]),
    ]
    for copy in small + copies:
        copy.start()
    for copy in small:
        copy.wait()
    wt = wt_ref[...]
    bias = to_column(bias_ref[...], bits)
    wa_even, ha_even = even("wa"), even("ha")
    mass = jnp.zeros((bits, 128), F32)
    keep = {}
    for r, copy in enumerate(copies):
        copy.wait()
        logits = dot(wt, x_ref[r].reshape(lanes, width), ((1,), (1,))) + bias
        squash = jax.nn.sigmoid(logits)
        sq_ref[r] = squash
        prob = prob_of(squash)
        for k in range(lanes // 128):
            mass += prob[:, k * 128 : (k + 1) * 128]
        left, right = logits[:, :edge].astype(BF), logits[:, lanes - edge :].astype(BF)
        ea_ref[r, :bits] = jnp.where(wa_even, right, left)
        eb_ref[r, :bits] = jnp.where(wa_even, left, right)
        if r < 2:
            keep[r] = logits.astype(BF)
        if r >= rows - 2:
            k = r - (rows - 2)
            top, bottom = keep[k], logits.astype(BF)
            ra_ref[k, :bits, edge : edge + lanes] = jnp.where(ha_even, bottom, top)
            rb_ref[k, :bits, edge : edge + lanes] = jnp.where(ha_even, top, bottom)
    row = to_row(jnp.sum(mass, axis=1, keepdims=True), bits)
    row = jnp.concatenate([row, jnp.zeros((1, edge - bits), F32)], axis=1)
    mass_ref[...] = row
    high = row.astype(BF).astype(F32)
    middle = (row - high).astype(BF).astype(F32)
    spare = ea_ref.shape[1] - bits
    parts = jnp.concatenate([high, middle, row - high - middle, jnp.zeros((spare - 3, edge), F32)], axis=0).astype(BF)
    ea_ref[0, bits:] = parts
    eb_ref[0, bits:] = parts


def encode(latents, wt, bit_bias):
    rows, cols, images, width = latents.shape
    bits = wt.shape[0]
    lanes, edge = cols * images, 2 * images
    padded = -(-(bits + 3) // 8) * 8
    shape = jax.ShapeDtypeStruct
    return pl.pallas_call(
        encode_kernel,
        in_specs=[HBM] * 3,
        out_specs=[VMEM] * 7,
        out_shape=[
            pltpu.VMEM(latents.shape, BF),
            shape((rows, bits, lanes), F32),
            shape((rows, padded, edge), BF),
            shape((rows, padded, edge), BF),
            shape((2, padded, lanes + 2 * edge), BF),
            shape((2, padded, lanes + 2 * edge), BF),
            shape((1, edge), F32),
        ],
        scratch_shapes=[pltpu.VMEM(wt.shape, BF), pltpu.VMEM(bit_bias.shape, F32), pltpu.SemaphoreType.DMA((rows + 2,))],
        compiler_params=params(8),
        cost_estimate=cost(2 * rows * lanes * width * 256, latents.size * 2),
        name="encode",
    )(latents, wt, bit_bias)


def pack_kernel(wa_a, wa_b, ra_ref, rb_ref, after, ra_out, rb_out):
    rows, _, edge = wa_a.shape
    lanes = ra_ref.shape[2] - 2 * edge
    wa_even, ha_even = even("wa"), even("ha")
    for k in range(2):
        ends = [(wa_a[r], wa_b[r]) for r in (k, rows - 2 + k)]
        (top_l, top_r), (bot_l, bot_r) = [(jnp.where(wa_even, b, a), jnp.where(wa_even, a, b)) for a, b in ends]
        for out, own, low in ((ra_out, ra_ref, ha_even), (rb_out, rb_ref, jnp.logical_not(ha_even))):
            out[k, :, edge : edge + lanes] = own[k, :, edge : edge + lanes]
            out[k, :, :edge] = jnp.where(low, bot_l, top_l)
            out[k, :, edge + lanes :] = jnp.where(low, bot_r, top_r)


def pack(wa_a, wa_b, ra, rb, after):
    return pl.pallas_call(
        pack_kernel,
        in_specs=[VMEM] * 4 + [pl.BlockSpec(memory_space=pl.ANY)],
        out_specs=[VMEM] * 2,
        out_shape=[jax.ShapeDtypeStruct(a.shape, a.dtype) for a in (ra, rb)],
        compiler_params=params(2),
        cost_estimate=cost(0, 2**18),
        name="pack",
    )(wa_a, wa_b, ra, rb, after)


def outward_kernel(first, x_hbm, w_ref, sq_ref, after, cg_ref, up_ref, x_ref, sem):
    rows, bits, lanes = cg_ref.shape
    width = x_hbm.shape[3]
    copies = [pltpu.make_async_copy(x_hbm.at[first + r], x_ref.at[r], sem.at[r]) for r in range(rows)]
    for copy in copies:
        copy.start()
    w = w_ref[...]
    total = jnp.zeros((bits, width), F32)
    for r, copy in enumerate(copies):
        copy.wait()
        x = x_ref[r].reshape(lanes, width)
        code = (2.0 * sq_ref[first + r] - 1.0).astype(BF)
        cg_ref[r] = dot(w, x, ((1,), (1,)))
        total += dot(code, x, ((1,), (0,)))
    up_ref[...] = total


def outward(cotangent, w_up, squash, first, rows, after):
    _, cols, images, width = cotangent.shape
    bits, lanes = w_up.shape[0], cols * images
    return pl.pallas_call(
        functools.partial(outward_kernel, first),
        in_specs=[HBM, VMEM, VMEM, pl.BlockSpec(memory_space=pl.ANY)],
        out_specs=[VMEM] * 2,
        out_shape=[jax.ShapeDtypeStruct((rows, bits, lanes), F32), jax.ShapeDtypeStruct((bits, width), F32)],
        scratch_shapes=[pltpu.VMEM((rows, cols, images, width), BF), pltpu.SemaphoreType.DMA((rows,))],
        compiler_params=params(12),
        cost_estimate=cost(4 * rows * lanes * width * 256, rows * lanes * width * 2),
        name="outward",
    )(cotangent, w_up, squash, after)


def row_of(refs, r):
    for ref in refs:
        if r < ref.shape[0]:
            return ref[r]
        r -= ref.shape[0]


def fill_row(pe, k, squash, left, right):
    lanes, edge = squash.shape[1], left.shape[1]
    pe[k, :, edge : edge + lanes] = prob_of(squash)
    pe[k, :, :edge] = prob_of(jax.nn.sigmoid(left.astype(F32)))
    pe[k, :, edge + lanes :] = prob_of(jax.nn.sigmoid(right.astype(F32)))


def slopes(pe, k, images):
    wide = pe.shape[2] - 2 * images
    t = pe[k] + pe[k + 1] + pe[k + 2]
    pooled = (t[:, :wide] + t[:, images : images + wide] + t[:, 2 * images :]) / 9.0
    lp, lq = jnp.log(pooled), jnp.log(1.0 - pooled)
    entropy = jnp.sum(pooled * (lq - lp) - lq, axis=0, keepdims=True)
    return local_weight * (lq - lp), entropy[:, images : wide - images]


def gradients(slope, squash, cg, g_ref, stacked, images):
    bits, lanes = squash.shape
    half = stacked.shape[0] // 2
    t = slope[0] + slope[1] + slope[2]
    spread = (t[:, :lanes] + t[:, images : images + lanes] + t[:, 2 * images :]) / 9.0
    steep = squash * (1.0 - squash)
    g = 2.0 * cg + 0.98 * spread
    g_ref[...] = g
    stacked[:bits] = (g * steep).astype(BF)
    stacked[half : half + bits] = steep.astype(BF)
    values = stacked[...]
    columns = values[:, :128].astype(F32)
    for k in range(1, lanes // 128):
        columns += values[:, k * 128 : (k + 1) * 128].astype(F32)
    return values, columns


def inner_kernel(x_ref, sq_ref, cg0_ref, cg1_ref, wa_a, wa_b, g_ref, slope_ref, ent_ref, acc_ref, columns_ref, pe, stacked):
    rows, bits, lanes = sq_ref.shape
    images, width = x_ref.shape[2:]
    wa_even = even("wa")
    stacked[...] = jnp.zeros_like(stacked)
    for k in range(rows):
        a, b = wa_a[k, :bits], wa_b[k, :bits]
        fill_row(pe, k, sq_ref[k], jnp.where(wa_even, b, a), jnp.where(wa_even, a, b))
    acc = jnp.zeros(acc_ref.shape, F32)
    columns = jnp.zeros(columns_ref.shape, F32)
    for r in range(1, rows - 1):
        slope_ref[r - 1], ent_ref[r : r + 1] = slopes(pe, r - 1, images)
        done = r - 1
        if done >= 2:
            values, sums = gradients(
                [slope_ref[done - 2], slope_ref[done - 1], slope_ref[done]], sq_ref[done], row_of((cg0_ref, cg1_ref), done), g_ref.at[done - 2], stacked.at[done % 2], images
            )
            acc += dot(values, x_ref[done].reshape(lanes, width), ((1,), (0,)))
            columns += sums
    ent_ref[0:1] = jnp.zeros((1, lanes), F32)
    ent_ref[rows - 1 : rows] = jnp.zeros((1, lanes), F32)
    acc_ref[...] = acc
    columns_ref[...] = columns


def inner(x, squash, cgs, wa_a, wa_b):
    images, width = x.shape[2:]
    rows, bits, lanes = squash.shape
    padded = -(-bits // 16) * 16
    shape = lambda *dims: jax.ShapeDtypeStruct(dims, F32)
    return pl.pallas_call(
        inner_kernel,
        in_specs=[VMEM] * 6,
        out_specs=[VMEM] * 5,
        out_shape=[
            shape(rows - 4, bits, lanes),
            shape(rows - 2, bits, lanes + 2 * images),
            shape(rows, lanes),
            shape(2 * padded, width),
            shape(2 * padded, 128),
        ],
        scratch_shapes=[pltpu.VMEM((rows, bits, lanes + 4 * images), F32), pltpu.VMEM((2, 2 * padded, lanes), BF)],
        compiler_params=params(8),
        cost_estimate=cost(2 * rows // 2 * lanes * width * 256, 2**20),
        name="inner",
    )(x, squash, *cgs, wa_a, wa_b)


def outer_kernel(
    x_ref, sq_ref, cg0_ref, cg1_ref, wa_a, wa_b, ha_a, ha_b, slope_ref, ent_in, acc_ref, columns_ref, up0_ref, up1_ref, mass_ref,
    g_ref, ent_ref, mine_ref, other_ref,
    pe, stacked,
):
    rows, bits, lanes = sq_ref.shape
    images, width = x_ref.shape[2:]
    half = stacked.shape[1] // 2
    wa_even, ha_even = even("wa"), even("ha")
    stacked[...] = jnp.zeros_like(stacked)
    for k in range(2):
        a, b = ha_a[k, :bits], ha_b[k, :bits]
        pe[k] = prob_of(jax.nn.sigmoid(jnp.where(ha_even, b, a).astype(F32)))
        pe[6 + k] = prob_of(jax.nn.sigmoid(jnp.where(ha_even, a, b).astype(F32)))
    for k, r in ((2, 0), (3, 1), (4, rows - 2), (5, rows - 1)):
        a, b = wa_a[r, :bits], wa_b[r, :bits]
        fill_row(pe, k, sq_ref[r], jnp.where(wa_even, b, a), jnp.where(wa_even, a, b))
    ent_ref[...] = ent_in[...]
    before, _ = slopes(pe, 0, images)
    first, ent_ref[0:1] = slopes(pe, 1, images)
    last, ent_ref[rows - 1 : rows] = slopes(pe, 4, images)
    after, _ = slopes(pe, 5, images)
    plans = (
        (0, (before, first, slope_ref[0])),
        (1, (first, slope_ref[0], slope_ref[1])),
        (rows - 2, (slope_ref[rows - 4], slope_ref[rows - 3], last)),
        (rows - 1, (slope_ref[rows - 3], last, after)),
    )
    acc, columns = acc_ref[...], columns_ref[...]
    for k, (r, around) in enumerate(plans):
        values, sums = gradients(around, sq_ref[r], row_of((cg0_ref, cg1_ref), r), g_ref.at[k], stacked.at[k % 2], images)
        acc += dot(values, x_ref[r].reshape(lanes, width), ((1,), (0,)))
        columns += sums
    total = jnp.sum(columns, axis=1, keepdims=True)
    others = sum(ref[0, bits:].astype(F32)[k : k + 1] for ref in (wa_a, wa_b) for k in range(3))
    rows_of = (to_row(total[:bits], bits), to_row(total[half : half + bits], bits), mass_ref[:, :bits], others[:, :bits])
    low, high = slice(0, width // 2), slice(width // 2, width)
    pieces = ((0, acc[:bits]), (bits, acc[half : half + bits]), (2 * bits, up0_ref[...] + up1_ref[...]))
    for ref, flip in ((mine_ref, False), (other_ref, True)):
        ref[3 * bits :, :] = jnp.zeros((ref.shape[0] - 3 * bits, ref.shape[1]), F32)
        take_low = jnp.logical_xor(ha_even, flip)
        for at, piece in pieces:
            ref[at : at + bits] = jnp.where(take_low, piece[:, low], piece[:, high])
        ref[3 * bits : 3 * bits + 1, :bits] = rows_of[0]
        ref[3 * bits : 3 * bits + 1, 128 : 128 + bits] = rows_of[1]
        ref[3 * bits + 1 : 3 * bits + 2, :bits] = rows_of[2]
        ref[3 * bits + 1 : 3 * bits + 2, 128 : 128 + bits] = rows_of[3]


def outer(x, squash, cgs, halos, inside, ups, mass):
    images, width = x.shape[2:]
    rows, bits, lanes = squash.shape
    padded = -(-bits // 16) * 16
    sums = -(-(3 * bits + 2) // 8) * 8
    shape = lambda *dims: jax.ShapeDtypeStruct(dims, F32)
    return pl.pallas_call(
        outer_kernel,
        in_specs=[VMEM] * 15,
        out_specs=[VMEM] * 4,
        out_shape=[shape(4, bits, lanes), shape(rows, lanes), shape(sums, width // 2), shape(sums, width // 2)],
        scratch_shapes=[pltpu.VMEM((8, bits, lanes + 4 * images), F32), pltpu.VMEM((2, 2 * padded, lanes), BF)],
        compiler_params=params(8),
        cost_estimate=cost(2 * 4 * lanes * width * 256, 2**20),
        name="outer",
    )(x, squash, *cgs, *halos, *inside, *ups, mass)


def back_kernel(count, first, slots, gi_ref, go_ref, sq_ref, wt_ref, *refs):
    sums, (out_hbm, out_ref, sem) = refs[: len(slots)], refs[-3:]
    rows, bits, _ = sq_ref.shape
    at = 3 * bits + 1
    marginal = sum(ref[at : at + 1, lane : lane + bits] for ref, lane in zip(sums, slots)) / count
    drift = to_column(0.98 * margin_weight * jnp.log((1.0 - marginal) / marginal), bits)
    wt = wt_ref[...]
    copies = [pltpu.make_async_copy(out_ref.at[k], out_hbm.at[first + k], sem.at[k]) for k in range(out_ref.shape[0])]
    for k, copy in enumerate(copies):
        r = first + k
        squash = sq_ref[r]
        g = gi_ref[r - 2] if 2 <= r < rows - 2 else go_ref[r if r < 2 else r - (rows - 4)]
        grad = ((g - drift) * (squash * (1.0 - squash))).astype(BF)
        out_ref[k] = dot(grad, wt, ((0,), (0,))).astype(BF).reshape(out_ref.shape[1:])
        copy.start()
    for copy in copies:
        copy.wait()


def back(shape, g_inner, g_outer, squash, wt, marginal, count, first, rows, onto=None):
    _, bits, lanes = squash.shape
    width = shape[3]
    arrays, slots = zip(*marginal)
    more = [] if onto is None else [onto]
    return pl.pallas_call(
        functools.partial(back_kernel, count, first, slots),
        in_specs=[VMEM] * (4 + len(arrays)) + [HBM] * len(more),
        out_specs=HBM,
        out_shape=jax.ShapeDtypeStruct(shape, BF),
        input_output_aliases={4 + len(arrays): 0} if more else {},
        scratch_shapes=[pltpu.VMEM((rows, *shape[1:]), BF), pltpu.SemaphoreType.DMA((rows,))],
        compiler_params=params(16),
        cost_estimate=cost(2 * rows * lanes * width * 256, rows * lanes * width * 2),
        name="back",
    )(g_inner, g_outer, squash, wt, *arrays, *more)


def finish_kernel(count, mine_ref, other_ref, marginal_ref, down_ref, bias_ref, up_ref):
    bits = marginal_ref.shape[1]
    core = even("ha")
    a, b = mine_ref[...], other_ref[...]
    sums = jnp.concatenate([jnp.where(core, a, b), jnp.where(core, b, a)], axis=1)
    mass = mine_ref[3 * bits + 1 : 3 * bits + 2, :bits]
    marginal = mass / count
    marginal_ref[...] = marginal
    drift_row = margin_weight * jnp.log((1.0 - marginal) / marginal)
    drift = to_column(drift_row, bits)
    down = (sums[:bits] - 0.98 * drift * sums[bits : 2 * bits]) / count
    down_ref[...] = down
    bias_ref[...] = (mine_ref[3 * bits : 3 * bits + 1, :bits] - 0.98 * drift_row * mine_ref[3 * bits : 3 * bits + 1, 128 : 128 + bits]) / count
    up_ref[...] = sums[2 * bits : 3 * bits] / count


def finish(mine, other, bits, count):
    width = 2 * mine.shape[1]
    return pl.pallas_call(
        functools.partial(finish_kernel, count),
        out_shape=[
            jax.ShapeDtypeStruct((1, bits), F32),
            jax.ShapeDtypeStruct((bits, width), F32),
            jax.ShapeDtypeStruct((1, bits), F32),
            jax.ShapeDtypeStruct((bits, width), F32),
        ],
        compiler_params=pltpu.CompilerParams(vmem_limit_bytes=8 * 2**20),
        name="finish",
    )(mine, other)


def swap(x, axis, mask):
    return lax.ppermute(x, axis, [(i, i ^ mask) for i in range(lax.axis_size(axis))])


def swap_outer(x, axis):
    count = lax.axis_size(axis)
    return lax.ppermute(x, axis, [(i, (((i + 1) ^ 1) - 1) % count) for i in range(count)])


def exchanged(x, axis, stride, radix):
    return [swap(x, axis, d * stride) for d in range(1, radix)]


def stages(count, stride):
    while stride < count:
        radix = 4 if stride * 4 <= count else 2
        yield stride, radix
        stride *= radix


def summed(x, axis, start):
    for stride, radix in stages(lax.axis_size(axis), start):
        x = sum(exchanged(x, axis, stride, radix), x)
    return x


def local(latents, cotangent, w_down, bit_bias, w_up):
    rows, cols, images, width = latents.shape
    bits = w_down.shape[1]
    columns = lax.axis_size("wa")
    count = rows * cols * images * lax.axis_size("ha") * columns
    wt = w_down.T
    near = lambda a: pltpu.with_memory_space_constraint(a, pltpu.HBM)
    latents, cotangent = near(latents), near(cotangent)
    x, squash, ea, eb, ra, rb, mass = encode(latents, near(wt), near(bit_bias.reshape(1, bits)))
    x = pltpu.with_memory_space_constraint(x, pltpu.VMEM)
    wa_a, wa_b = swap(ea, "wa", 1), swap_outer(eb, "wa")
    part = rows // 2
    cg0, up0 = outward(cotangent, w_up, squash, 0, part, mass)
    ra, rb = pack(wa_a, wa_b, ra, rb, up0)
    ha_a, ha_b = swap(ra, "ha", 1), swap_outer(rb, "ha")
    cg1, up1 = outward(cotangent, w_up, squash, part, rows - part, ra)
    g_inner, *inside = inner(x, squash, (cg0, cg1), wa_a, wa_b)
    g_outer, entropy, mine, other = outer(x, squash, (cg0, cg1), (wa_a, wa_b, ha_a, ha_b), inside, (up0, up1), mass)
    sums = mine + swap(other, "ha", 1)
    sums = summed(sums, "ha", 2)
    run = functools.partial(back, latents.shape, g_inner, g_outer, squash, wt)
    if columns == 4:
        opposite, *rest = [swap(sums, "wa", d) for d in (2, 1, 3)]
        grad_latents = run([(sums, 0), (sums, 128), (opposite, 0)], count, 0, part)
        near_sums, grad_latents = lax.optimization_barrier((sums + opposite, grad_latents))
        sums = sum(rest, near_sums)
    else:
        sums = summed(sums, "wa", 1)
        grad_latents = run([(sums, 0)], count, 0, part)
    partner = swap(sums, "ha", 1)
    grad_latents = run([(sums, 0)], count, part, rows - part, grad_latents)
    marginal, grad_down, grad_bias, grad_up = finish(sums, partner, bits, count)
    return (
        grad_latents,
        entropy.reshape(rows, cols, images),
        marginal.reshape(bits),
        grad_down.T,
        grad_bias.reshape(bits),
        grad_up,
    )


def solution(mesh):
    placed = (P("ha", "wa", None, None), P("ha", "wa", None, None), P(), P(), P())
    return jax.shard_map(
        local,
        mesh=mesh,
        in_specs=placed,
        out_specs=(P("ha", "wa", None, None), P("ha", "wa", None), P(), P(), P(), P()),
        check_vma=False,
    )
```

```python
import functools

import jax
import jax.numpy as jnp
from jax import lax
from jax.experimental import pallas as pl
from jax.experimental.pallas import tpu as pltpu
from jax.sharding import PartitionSpec as P

local_weight = 4.0
margin_weight = 4.0
BF, F32 = jnp.bfloat16, jnp.float32
EARLY_ROWS, FIRST_ROWS = 2, 6


VMEM = pl.BlockSpec(memory_space=pltpu.VMEM)
HBM = pl.BlockSpec(memory_space=pltpu.HBM)


def params(mib):
    return pltpu.CompilerParams(vmem_limit_bytes=mib * 2**20)


def cost(flops, bytes_accessed):
    return pl.CostEstimate(flops=flops, bytes_accessed=bytes_accessed, transcendentals=0)


def dot(a, b, dims):
    return lax.dot_general(a, b, (dims, ((), ())), preferred_element_type=F32)


def to_column(row, n):
    eye = lax.broadcasted_iota(jnp.int32, (n, n), 0) == lax.broadcasted_iota(jnp.int32, (n, n), 1)
    return jnp.sum(jnp.where(eye, row, 0.0), axis=1, keepdims=True)


def to_row(column, n):
    eye = lax.broadcasted_iota(jnp.int32, (n, n), 0) == lax.broadcasted_iota(jnp.int32, (n, n), 1)
    return jnp.sum(jnp.where(eye, column, 0.0), axis=0, keepdims=True)


def even(axis):
    return lax.rem(lax.axis_index(axis), 2) == 0


def prob_of(squash):
    return 0.01 + 0.98 * squash


def spaced(shape, dtype=F32):
    return jax.ShapeDtypeStruct(shape, dtype)


def border(r, rows):
    return r if r < 2 else r - (rows - 4) if r >= rows - 2 else None


def row_of(edge_ref, middle_ref, r, rows):
    k = border(r, rows)
    return middle_ref[r - 2] if k is None else edge_ref[k]


def split_row(edge_ref, middle_ref, r, count):
    return edge_ref[r] if r < count else middle_ref[r - count]


def logits_of(x, wt, bias):
    return dot(wt, x.reshape(-1, x.shape[-1]), ((1,), (1,))) + bias


def add_mass(mass, squash):
    prob = prob_of(squash)
    for k in range(prob.shape[1] // 128):
        mass += prob[:, k * 128 : (k + 1) * 128]
    return mass


def put_edges(ea_ref, eb_ref, k, logits, edge, wa_even):
    bits, lanes = logits.shape
    left, right = logits[:, :edge].astype(BF), logits[:, lanes - edge :].astype(BF)
    ea_ref[k, :bits] = jnp.where(wa_even, right, left)
    eb_ref[k, :bits] = jnp.where(wa_even, left, right)


def encode_kernel(x_hbm, wt_hbm, bias_hbm, x_ref, sq_ref, ea_ref, eb_ref, ra_ref, rb_ref, mass_ref, wt_ref, bias_ref, sem):
    rows, bits = x_hbm.shape[0], sq_ref.shape[1]
    edge = 2 * x_hbm.shape[2]
    order = (0, 1, rows - 2, rows - 1)
    small = [pltpu.make_async_copy(wt_hbm, wt_ref, sem.at[4]), pltpu.make_async_copy(bias_hbm, bias_ref, sem.at[5])]
    copies = [pltpu.make_async_copy(x_hbm.at[r], x_ref.at[k], sem.at[k]) for k, r in enumerate(order)]
    for copy in small + copies:
        copy.start()
    for copy in small:
        copy.wait()
    wt, bias = wt_ref[...], to_column(bias_ref[...], bits)
    wa_even, ha_even = even("wa"), even("ha")
    mass = jnp.zeros((bits, 128), F32)
    packed = []
    for k, copy in enumerate(copies):
        copy.wait()
        logits = logits_of(x_ref[k], wt, bias)
        squash = jax.nn.sigmoid(logits)
        sq_ref[k] = squash
        mass = add_mass(mass, squash)
        put_edges(ea_ref, eb_ref, k, logits, edge, wa_even)
        packed.append(logits.astype(BF))
        if k >= 2:
            ra_ref[k - 2, :bits] = jnp.where(ha_even, packed[k], packed[k - 2])
            rb_ref[k - 2, :bits] = jnp.where(ha_even, packed[k - 2], packed[k])
    mass_ref[...] = mass


def encode(latents, wt, bit_bias, padded):
    _, cols, images, width = latents.shape
    bits = wt.shape[0]
    lanes, edge = cols * images, 2 * images
    return pl.pallas_call(
        encode_kernel,
        in_specs=[HBM] * 3,
        out_specs=[VMEM] * 9,
        out_shape=[
            pltpu.VMEM((4, cols, images, width), BF),
            spaced((4, bits, lanes)),
            spaced((4, padded, edge), BF),
            spaced((4, padded, edge), BF),
            spaced((2, padded, lanes), BF),
            spaced((2, padded, lanes), BF),
            spaced((bits, 128)),
            spaced(wt.shape, BF),
            spaced(bit_bias.shape),
        ],
        scratch_shapes=[pltpu.SemaphoreType.DMA((6,))],
        compiler_params=params(8),
        cost_estimate=cost(2 * 4 * lanes * width * 256, 4 * lanes * width * 2),
        name="encode",
    )(latents, wt, bit_bias)


def outward_row(x, w, squash, total):
    x = x.reshape(-1, x.shape[-1])
    code = (2.0 * squash - 1.0).astype(BF)
    return dot(w, x, ((1,), (1,))), total + dot(code, x, ((1,), (0,)))


def middle_kernel(
    x_hbm, c_hbm, wt_ref, bias_ref, up_w_ref, sqe_ref, mass_in,
    x_ref, sq_ref, ea_ref, eb_ref, mass_ref, cg_ref, up_ref,
    c_ref, sem,
):
    rows, (inside, bits, lanes), early = x_hbm.shape[0], sq_ref.shape, cg_ref.shape[0]
    edge = 2 * x_hbm.shape[2]
    copies = [pltpu.make_async_copy(x_hbm.at[2 + k], x_ref.at[k], sem.at[k]) for k in range(inside)]
    outward = [pltpu.make_async_copy(c_hbm.at[k], c_ref.at[k], sem.at[inside + k]) for k in range(early)]
    for copy in copies + outward:
        copy.start()
    wt, bias = wt_ref[...], to_column(bias_ref[...], bits)
    wa_even = even("wa")
    mass = mass_in[...]
    for k, copy in enumerate(copies):
        copy.wait()
        logits = logits_of(x_ref[k], wt, bias)
        squash = jax.nn.sigmoid(logits)
        sq_ref[k] = squash
        mass = add_mass(mass, squash)
        put_edges(ea_ref, eb_ref, k, logits, edge, wa_even)
    row = to_row(jnp.sum(mass, axis=1, keepdims=True), bits)
    mass_ref[...] = jnp.concatenate([row, jnp.zeros((1, 128 - bits), F32)], axis=1)
    total = jnp.zeros(up_ref.shape, F32)
    for k, copy in enumerate(outward):
        copy.wait()
        cg_ref[k], total = outward_row(c_ref[k], up_w_ref[...], row_of(sqe_ref, sq_ref, k, rows), total)
    up_ref[...] = total


def middle(latents, cotangent, wt, bias, w_up, squash, mass, padded, early):
    rows, cols, images, width = latents.shape
    bits, lanes, edge = wt.shape[0], cols * images, 2 * images
    inside = rows - 4
    return pl.pallas_call(
        middle_kernel,
        in_specs=[HBM] * 2 + [VMEM] * 5,
        out_specs=[VMEM] * 7,
        out_shape=[
            pltpu.VMEM((inside, cols, images, width), BF),
            spaced((inside, bits, lanes)),
            spaced((inside, padded, edge), BF),
            spaced((inside, padded, edge), BF),
            spaced((1, 128)),
            spaced((early, bits, lanes)),
            spaced((bits, width)),
        ],
        scratch_shapes=[pltpu.VMEM((early, cols, images, width), BF), pltpu.SemaphoreType.DMA((inside + early,))],
        compiler_params=params(12),
        cost_estimate=cost(2 * (inside + 2 * early) * lanes * width * 256, (inside + early) * lanes * width * 2),
        name="middle",
    )(latents, cotangent, wt, bias, w_up, squash, mass)


def pack_kernel(ea_e, eb_e, ea_m, eb_m, ha_a, ha_b, mass_ref, ea_ref, eb_ref):
    rows, _, edge = ea_ref.shape
    rows -= 5
    lanes = ha_a.shape[2]
    spare = 8
    wa_even, ha_even = even("wa"), even("ha")
    for out, outer, inner in ((ea_ref, ea_e, ea_m), (eb_ref, eb_e, eb_m)):
        for k in range(2):
            out[2 + k] = outer[k]
            out[rows + k] = outer[2 + k]
        for k in range(rows - 4):
            out[4 + k] = inner[k]
    for k in range(2):
        for at, side in ((k, jnp.where(ha_even, ha_b[k], ha_a[k])), (rows + 2 + k, jnp.where(ha_even, ha_a[k], ha_b[k]))):
            left, right = side[:, :edge], side[:, lanes - edge :]
            ea_ref[at] = jnp.where(wa_even, right, left)
            eb_ref[at] = jnp.where(wa_even, left, right)
    row = mass_ref[...]
    high = row.astype(BF).astype(F32)
    middle = (row - high).astype(BF).astype(F32)
    parts = jnp.concatenate([high, middle, row - high - middle, jnp.zeros((spare - 3, edge), F32)], axis=0).astype(BF)
    ea_ref[rows + 4, :spare] = parts
    eb_ref[rows + 4, :spare] = parts


def pack(edges, halos, mass, rows):
    _, padded, edge = edges[0].shape
    return pl.pallas_call(
        pack_kernel,
        in_specs=[VMEM] * 7,
        out_specs=[VMEM] * 2,
        out_shape=[spaced((rows + 5, padded, edge), BF)] * 2,
        compiler_params=params(2),
        cost_estimate=cost(0, 2**18),
        name="pack",
    )(*edges, *halos, mass)


def window(t, cell):
    wide = t.shape[1] - 2 * cell
    return (t[:, :wide] + t[:, cell : cell + wide] + t[:, 2 * cell :]) / 9.0


def slope_of(t, cell):
    pooled = window(t, cell)
    lp, lq = jnp.log(pooled), jnp.log(1.0 - pooled)
    return local_weight * (lq - lp), jnp.sum(pooled * (lq - lp) - lq, axis=0, keepdims=True)


def gradients(t, cell, squash, cg, stacked):
    bits, lanes = squash.shape
    half = stacked.shape[0] // 2
    steep = squash * (1.0 - squash)
    g = 2.0 * cg + 0.98 * window(t, cell)
    stacked[:bits] = (g * steep).astype(BF)
    stacked[half : half + bits] = steep.astype(BF)
    values = stacked[...]
    columns = values[:, :128].astype(F32)
    for k in range(1, lanes // 128):
        columns += values[:, k * 128 : (k + 1) * 128].astype(F32)
    return g, values, columns


def inner_kernel(
    c_hbm, xe_ref, xm_ref, sqe_ref, sqm_ref, ha_a, ha_b, cg_in, up_in, up_w_ref, after,
    cg_ref, up_ref, g_ref, slope_ref, ent_ref, acc_ref, columns_ref, pe_ref,
    c_ref, stacked, sem,
):
    late, bits, lanes = cg_ref.shape
    early, rows = cg_in.shape[0], g_ref.shape[0]
    images, width = xe_ref.shape[2:]
    edge = 2 * images
    copies = [pltpu.make_async_copy(c_hbm.at[early + k], c_ref.at[k], sem.at[k]) for k in range(late)]
    for copy in copies:
        copy.start()
    ha_even = even("ha")
    stacked[...] = jnp.zeros_like(stacked)
    for k in range(2):
        a, b = ha_a[k, :bits], ha_b[k, :bits]
        pe_ref[k] = prob_of(jax.nn.sigmoid(jnp.where(ha_even, b, a).astype(F32)))
        pe_ref[rows + 2 + k] = prob_of(jax.nn.sigmoid(jnp.where(ha_even, a, b).astype(F32)))
    for r in range(rows):
        pe_ref[2 + r] = prob_of(row_of(sqe_ref, sqm_ref, r, rows))
    for e in range(rows + 2):
        slope_ref[e], entropy = slope_of(pe_ref[e] + pe_ref[e + 1] + pe_ref[e + 2], images)
        if 1 <= e <= rows:
            ent_ref[e - 1 : e] = entropy
    total = up_in[...]
    acc = jnp.zeros(acc_ref.shape, F32)
    columns = jnp.zeros(columns_ref.shape, F32)
    for r in range(rows):
        squash = row_of(sqe_ref, sqm_ref, r, rows)
        if r < early:
            cg = cg_in[r]
        else:
            copies[r - early].wait()
            cg, total = outward_row(c_ref[r - early], up_w_ref[...], squash, total)
            cg_ref[r - early] = cg
        t = slope_ref[r] + slope_ref[r + 1] + slope_ref[r + 2]
        g_ref[r], values, sums = gradients(t, images, squash[:, edge : lanes - edge], cg[:, edge : lanes - edge], stacked.at[r % 2])
        x = row_of(xe_ref, xm_ref, r, rows)[2:-2].reshape(lanes - 2 * edge, width)
        acc += dot(values, x, ((1,), (0,)))
        columns += sums
    acc_ref[...] = acc
    columns_ref[...] = columns
    up_ref[...] = total


def inner(cotangent, x_edge, x_middle, sq_edge, sq_middle, ha_a, ha_b, cg, up, w_up, after):
    rows, cols, images, width = cotangent.shape
    early, bits, lanes = cg.shape
    late, edge = rows - early, 2 * images
    padded = -(-bits // 16) * 16
    return pl.pallas_call(
        inner_kernel,
        in_specs=[HBM] + [VMEM] * 9 + [pl.BlockSpec(memory_space=pl.ANY)],
        out_specs=[VMEM] * 8,
        out_shape=[
            spaced((late, bits, lanes)),
            spaced((bits, width)),
            spaced((rows, bits, lanes - 2 * edge)),
            spaced((rows + 2, bits, lanes - edge)),
            spaced((rows, lanes - edge)),
            spaced((2 * padded, width)),
            spaced((2 * padded, 128)),
            spaced((rows + 4, bits, lanes)),
        ],
        scratch_shapes=[
            pltpu.VMEM((late, cols, images, width), BF),
            pltpu.VMEM((2, 2 * padded, lanes - 2 * edge), BF),
            pltpu.SemaphoreType.DMA((late,)),
        ],
        compiler_params=params(12),
        cost_estimate=cost(2 * (2 * late + rows) * lanes * width * 256, late * lanes * width * 2),
        name="inner",
    )(cotangent, x_edge, x_middle, sq_edge, sq_middle, ha_a, ha_b, cg, up, w_up, after)


def outer_kernel(
    xe_ref, xm_ref, sqe_ref, sqm_ref, cg0_ref, cg1_ref, wa_a, wa_b, slope_ref, pe_ref, acc_in, columns_in, up_ref, mass_ref,
    g_ref, ent_ref, mine_ref, other_ref,
    near, stacked,
):
    rows, bits, _ = g_ref.shape
    images, width = xe_ref.shape[2:]
    lanes, edge = sqe_ref.shape[2], 2 * images
    half = stacked.shape[1] // 2
    wa_even, ha_even = even("wa"), even("ha")
    stacked[...] = jnp.zeros_like(stacked)
    ends = lambda v: jnp.concatenate([v[:, :edge], v[:, lanes - edge :]], axis=1)
    probs = []
    for e in range(rows + 4):
        a, b = wa_a[e, :bits], wa_b[e, :bits]
        left = prob_of(jax.nn.sigmoid(jnp.where(wa_even, b, a).astype(F32)))
        right = prob_of(jax.nn.sigmoid(jnp.where(wa_even, a, b).astype(F32)))
        own = pe_ref[e]
        probs.append((jnp.concatenate([left, own[:, :edge]], axis=1), jnp.concatenate([own[:, lanes - edge :], right], axis=1)))
    for e in range(rows + 2):
        sides = [probs[e][i] + probs[e + 1][i] + probs[e + 2][i] for i in range(2)]
        (left, left_ent), (right, right_ent) = [slope_of(t, images) for t in sides]
        if 1 <= e <= rows:
            ent_ref[e - 1 : e] = jnp.concatenate([left_ent[:, images:], right_ent[:, :images]], axis=1)
        inside = slope_ref[e]
        near[e, 0] = jnp.concatenate([left, inside[:, :edge]], axis=1)
        near[e, 1] = jnp.concatenate([inside[:, lanes - 2 * edge :], right], axis=1)
    acc, columns = acc_in[...], columns_in[...]
    for r in range(rows):
        squash, cg = ends(row_of(sqe_ref, sqm_ref, r, rows)), ends(split_row(cg0_ref, cg1_ref, r, cg0_ref.shape[0]))
        x = row_of(xe_ref, xm_ref, r, rows)
        x = jnp.concatenate([x[:2].reshape(edge, width), x[-2:].reshape(edge, width)], axis=0)
        spread = jnp.concatenate([window(near[r, i] + near[r + 1, i] + near[r + 2, i], images) for i in range(2)], axis=1)
        steep = squash * (1.0 - squash)
        g = 2.0 * cg + 0.98 * spread
        g_ref[r] = g
        at = stacked.at[r % 2]
        at[:bits] = (g * steep).astype(BF)
        at[half : half + bits] = steep.astype(BF)
        values = at[...]
        acc += dot(values, x, ((1,), (0,)))
        for k in range(2 * edge // 128):
            columns += values[:, k * 128 : (k + 1) * 128].astype(F32)
    total = jnp.sum(columns, axis=1, keepdims=True)
    others = sum(ref[rows + 4, :8].astype(F32)[k : k + 1] for ref in (wa_a, wa_b) for k in range(3))
    rows_of = (to_row(total[:bits], bits), to_row(total[half : half + bits], bits), mass_ref[:, :bits], others[:, :bits])
    low, high = slice(0, width // 2), slice(width // 2, width)
    pieces = ((0, acc[:bits]), (bits, acc[half : half + bits]), (2 * bits, up_ref[...]))
    lead = 3 * bits
    for ref, flip in ((mine_ref, False), (other_ref, True)):
        ref[lead:, :] = jnp.zeros((ref.shape[0] - lead, ref.shape[1]), F32)
        take_low = jnp.logical_xor(ha_even, flip)
        for at, piece in pieces:
            ref[at : at + bits] = jnp.where(take_low, piece[:, low], piece[:, high])
        ref[lead : lead + 1, :bits] = rows_of[0]
        ref[lead : lead + 1, 128 : 128 + bits] = rows_of[1]
        ref[lead + 1 : lead + 2, :bits] = rows_of[2]
        ref[lead + 1 : lead + 2, 128 : 128 + bits] = rows_of[3]


def outer(rows, width, images, *operands):
    bits = operands[2].shape[1]
    padded = -(-bits // 16) * 16
    sums = -(-(3 * bits + 2) // 8) * 8
    edge = 2 * images
    return pl.pallas_call(
        outer_kernel,
        in_specs=[VMEM] * len(operands),
        out_specs=[VMEM] * 4,
        out_shape=[spaced((rows, bits, 2 * edge)), spaced((rows, edge)), spaced((sums, width // 2)), spaced((sums, width // 2))],
        scratch_shapes=[pltpu.VMEM((rows + 2, 2, bits, 2 * edge), F32), pltpu.VMEM((2, 2 * padded, 2 * edge), BF)],
        compiler_params=params(8),
        cost_estimate=cost(2 * rows * 2 * edge * width * 256, 2**20),
        name="outer",
    )(*operands)


def back_kernel(count, first, slots, with_entropy, gi_ref, go_ref, sqe_ref, sqm_ref, wt_ref, *refs):
    sums, refs = refs[: len(slots)], refs[len(slots) :]
    rows, bits, edge = go_ref.shape
    edge //= 2
    extra = []
    if with_entropy:
        ei_ref, eo_ref, out_hbm, ent_hbm, out_ref, sem, ent_ref, ent_sem = refs
        images = ent_ref.shape[2]
        for c in range(ent_ref.shape[1]):
            at = (c - 1) * images
            last = c == ent_ref.shape[1] - 1
            ent_ref[:, c, :] = ei_ref[:, at : at + images] if c > 0 and not last else eo_ref[:, images:] if last else eo_ref[:, :images]
        extra = [pltpu.make_async_copy(ent_ref, ent_hbm, ent_sem)]
        extra[0].start()
    else:
        _, out_hbm, out_ref, sem = refs
    at = 3 * bits + 1
    marginal = sum(ref[at : at + 1, lane : lane + bits] for ref, lane in zip(sums, slots)) / count
    drift = to_column(0.98 * margin_weight * jnp.log((1.0 - marginal) / marginal), bits)
    wt = wt_ref[...]
    copies = [pltpu.make_async_copy(out_ref.at[k], out_hbm.at[first + k], sem.at[k]) for k in range(out_ref.shape[0])]
    for k, copy in enumerate(copies):
        r = first + k
        squash = row_of(sqe_ref, sqm_ref, r, rows)
        g = jnp.concatenate([go_ref[r][:, :edge], gi_ref[r], go_ref[r][:, edge:]], axis=1)
        grad = ((g - drift) * (squash * (1.0 - squash))).astype(BF)
        out_ref[k] = dot(grad, wt, ((0,), (0,))).astype(BF).reshape(out_ref.shape[1:])
        copy.start()
    for copy in copies + extra:
        copy.wait()


def back(shape, g_inner, g_outer, sq_edge, sq_middle, wt, marginal, count, first, rows, entropies=(), onto=()):
    arrays, slots = zip(*marginal)
    operands = [g_inner, g_outer, sq_edge, sq_middle, wt, *arrays, *entropies]
    outs, scratch = [spaced(shape, BF)], [pltpu.VMEM((rows, *shape[1:]), BF), pltpu.SemaphoreType.DMA((rows,))]
    if entropies:
        outs.append(spaced(shape[:3]))
        scratch += [pltpu.VMEM(shape[:3], F32), pltpu.SemaphoreType.DMA]
    cells = rows * shape[1] * shape[2] * shape[3]
    return pl.pallas_call(
        functools.partial(back_kernel, count, first, slots, bool(entropies)),
        in_specs=[VMEM] * len(operands) + [HBM] * len(onto),
        out_specs=[HBM] * len(outs),
        out_shape=outs,
        input_output_aliases={len(operands): 0} if onto else {},
        scratch_shapes=scratch,
        compiler_params=params(16),
        cost_estimate=cost(2 * cells * 256, cells * 2),
        name="back",
    )(*operands, *onto)


def finish_kernel(count, mine_ref, other_ref, marginal_ref, down_ref, bias_ref, up_ref):
    bits = marginal_ref.shape[1]
    core = even("ha")
    a, b = mine_ref[...], other_ref[...]
    sums = jnp.concatenate([jnp.where(core, a, b), jnp.where(core, b, a)], axis=1)
    mass = mine_ref[3 * bits + 1 : 3 * bits + 2, :bits]
    marginal = mass / count
    marginal_ref[...] = marginal
    drift_row = margin_weight * jnp.log((1.0 - marginal) / marginal)
    drift = to_column(drift_row, bits)
    down = (sums[:bits] - 0.98 * drift * sums[bits : 2 * bits]) / count
    down_ref[...] = down
    bias_ref[...] = (mine_ref[3 * bits : 3 * bits + 1, :bits] - 0.98 * drift_row * mine_ref[3 * bits : 3 * bits + 1, 128 : 128 + bits]) / count
    up_ref[...] = sums[2 * bits : 3 * bits] / count


def finish(mine, other, bits, count):
    width = 2 * mine.shape[1]
    return pl.pallas_call(
        functools.partial(finish_kernel, count),
        out_shape=[
            jax.ShapeDtypeStruct((1, bits), F32),
            jax.ShapeDtypeStruct((bits, width), F32),
            jax.ShapeDtypeStruct((1, bits), F32),
            jax.ShapeDtypeStruct((bits, width), F32),
        ],
        compiler_params=pltpu.CompilerParams(vmem_limit_bytes=8 * 2**20),
        name="finish",
    )(mine, other)


def swap(x, axis, mask):
    return lax.ppermute(x, axis, [(i, i ^ mask) for i in range(lax.axis_size(axis))])


def swap_outer(x, axis):
    count = lax.axis_size(axis)
    return lax.ppermute(x, axis, [(i, (((i + 1) ^ 1) - 1) % count) for i in range(count)])


def exchanged(x, axis, stride, radix):
    return [swap(x, axis, d * stride) for d in range(1, radix)]


def stages(count, stride):
    while stride < count:
        radix = 4 if stride * 4 <= count else 2
        yield stride, radix
        stride *= radix


def summed(x, axis, start):
    for stride, radix in stages(lax.axis_size(axis), start):
        x = sum(exchanged(x, axis, stride, radix), x)
    return x


def local(latents, cotangent, w_down, bit_bias, w_up):
    rows, cols, images, width = latents.shape
    bits = w_down.shape[1]
    columns = lax.axis_size("wa")
    count = rows * cols * images * lax.axis_size("ha") * columns
    padded = -(-bits // 8) * 8
    early, first = EARLY_ROWS, FIRST_ROWS
    near = lambda a: pltpu.with_memory_space_constraint(a, pltpu.HBM)
    resident = lambda a: pltpu.with_memory_space_constraint(a, pltpu.VMEM)
    latents, cotangent = near(latents), near(cotangent)
    x_e, sq_e, ea_e, eb_e, ra, rb, mass, wt, bias = encode(latents, near(w_down.T), near(bit_bias.reshape(1, bits)), padded)
    ha_a, ha_b = swap(ra, "ha", 1), swap_outer(rb, "ha")
    x_m, sq_m, ea_m, eb_m, mass, cg0, up = middle(latents, cotangent, wt, bias, w_up, sq_e, mass, padded, early)
    x_e, x_m = resident(x_e), resident(x_m)
    ea, eb = pack((ea_e, eb_e, ea_m, eb_m), (ha_a, ha_b), mass, rows)
    wa_a, wa_b = swap(ea, "wa", 1), swap_outer(eb, "wa")
    cg1, up, g_inner, slope, ent_inner, acc, sums, probs = inner(cotangent, x_e, x_m, sq_e, sq_m, ha_a, ha_b, cg0, up, w_up, ea)
    g_outer, ent_outer, mine, other = outer(
        rows, width, images, x_e, x_m, sq_e, sq_m, cg0, cg1, wa_a, wa_b, slope, probs, acc, sums, up, mass
    )
    sums = mine + swap(other, "ha", 1)
    sums = summed(sums, "ha", 2)
    run = functools.partial(back, latents.shape, g_inner, g_outer, sq_e, sq_m, wt)
    if columns == 4:
        opposite, *rest = [swap(sums, "wa", d) for d in (2, 1, 3)]
        known = [(sums, 0), (sums, 128), (opposite, 0)]
        grad_latents, entropy = run(known, count, 0, first, entropies=(ent_inner, ent_outer))
        near_sums, grad_latents = lax.optimization_barrier((sums + opposite, grad_latents))
        sums = sum(rest, near_sums)
    else:
        sums = summed(sums, "wa", 1)
        grad_latents, entropy = run([(sums, 0)], count, 0, first, entropies=(ent_inner, ent_outer))
    partner = swap(sums, "ha", 1)
    (grad_latents,) = run([(sums, 0)], count, first, rows - first, onto=(grad_latents,))
    marginal, grad_down, grad_bias, grad_up = finish(sums, partner, bits, count)
    return grad_latents, entropy, marginal.reshape(bits), grad_down.T, grad_bias.reshape(bits), grad_up


def solution(mesh):
    placed = (P("ha", "wa", None, None), P("ha", "wa", None, None), P(), P(), P())
    return jax.shard_map(
        local,
        mesh=mesh,
        in_specs=placed,
        out_specs=(P("ha", "wa", None, None), P("ha", "wa", None), P(), P(), P(), P()),
        check_vma=False,
    )
```

```python
import functools

import jax
import jax.numpy as jnp
from jax import lax
from jax.experimental import pallas as pl
from jax.experimental.pallas import tpu as pltpu
from jax.sharding import PartitionSpec as P

local_weight = 4.0
margin_weight = 4.0
BF, F32 = jnp.bfloat16, jnp.float32
EARLY_ROWS, FIRST_ROWS, AHEAD_ROWS = 4, 6, 2


VMEM = pl.BlockSpec(memory_space=pltpu.VMEM)
HBM = pl.BlockSpec(memory_space=pltpu.HBM)


def params(mib):
    return pltpu.CompilerParams(vmem_limit_bytes=mib * 2**20)


def cost(flops, bytes_accessed):
    return pl.CostEstimate(flops=flops, bytes_accessed=bytes_accessed, transcendentals=0)


def dot(a, b, dims):
    return lax.dot_general(a, b, (dims, ((), ())), preferred_element_type=F32)


def to_column(row, n):
    eye = lax.broadcasted_iota(jnp.int32, (n, n), 0) == lax.broadcasted_iota(jnp.int32, (n, n), 1)
    return jnp.sum(jnp.where(eye, row, 0.0), axis=1, keepdims=True)


def to_row(column, n):
    eye = lax.broadcasted_iota(jnp.int32, (n, n), 0) == lax.broadcasted_iota(jnp.int32, (n, n), 1)
    return jnp.sum(jnp.where(eye, column, 0.0), axis=0, keepdims=True)


def even(axis):
    return lax.rem(lax.axis_index(axis), 2) == 0


def prob_of(squash):
    return 0.01 + 0.98 * squash


def spaced(shape, dtype=F32):
    return jax.ShapeDtypeStruct(shape, dtype)


def border(r, rows):
    return r if r < 2 else r - (rows - 4) if r >= rows - 2 else None


def latent_row(edge_ref, ahead_ref, middle_ref, r, rows):
    k = border(r, rows)
    return edge_ref[k] if k is not None else split_row(ahead_ref, middle_ref, r - 2, ahead_ref.shape[0])


def row_of(edge_ref, middle_ref, r, rows):
    k = border(r, rows)
    return middle_ref[r - 2] if k is None else edge_ref[k]


def split_row(edge_ref, middle_ref, r, count):
    return edge_ref[r] if r < count else middle_ref[r - count]


def logits_of(x, wt, bias):
    return dot(wt, x.reshape(-1, x.shape[-1]), ((1,), (1,))) + bias


def add_mass(mass, squash):
    prob = prob_of(squash)
    for k in range(prob.shape[1] // 128):
        mass += prob[:, k * 128 : (k + 1) * 128]
    return mass


def put_edges(ea_ref, eb_ref, k, logits, edge, wa_even):
    bits, lanes = logits.shape
    left, right = logits[:, :edge].astype(BF), logits[:, lanes - edge :].astype(BF)
    ea_ref[k, :bits] = jnp.where(wa_even, right, left)
    eb_ref[k, :bits] = jnp.where(wa_even, left, right)


def encode_kernel(x_hbm, wt_hbm, bias_hbm, x_ref, sq_ref, ea_ref, eb_ref, ra_ref, rb_ref, mass_ref, wt_ref, bias_ref, ahead_ref, sem):
    rows, bits = x_hbm.shape[0], sq_ref.shape[1]
    edge = 2 * x_hbm.shape[2]
    order = (0, 1, rows - 2, rows - 1, *range(2, 2 + ahead_ref.shape[0]))
    small = [pltpu.make_async_copy(wt_hbm, wt_ref, sem.at[4]), pltpu.make_async_copy(bias_hbm, bias_ref, sem.at[5])]
    place = lambda k: x_ref.at[k] if k < 4 else ahead_ref.at[k - 4]
    copies = [pltpu.make_async_copy(x_hbm.at[r], place(k), sem.at[k if k < 4 else k + 2]) for k, r in enumerate(order)]
    copies, ahead = copies[:4], copies[4:]
    for copy in small + copies + ahead:
        copy.start()
    for copy in small:
        copy.wait()
    wt, bias = wt_ref[...], to_column(bias_ref[...], bits)
    wa_even, ha_even = even("wa"), even("ha")
    mass = jnp.zeros((bits, 128), F32)
    packed = []
    for k, copy in enumerate(copies):
        copy.wait()
        logits = logits_of(x_ref[k], wt, bias)
        squash = jax.nn.sigmoid(logits)
        sq_ref[k] = squash
        mass = add_mass(mass, squash)
        put_edges(ea_ref, eb_ref, k, logits, edge, wa_even)
        packed.append(logits.astype(BF))
        if k >= 2:
            ra_ref[k - 2, :bits] = jnp.where(ha_even, packed[k], packed[k - 2])
            rb_ref[k - 2, :bits] = jnp.where(ha_even, packed[k - 2], packed[k])
    mass_ref[...] = mass
    for copy in ahead:
        copy.wait()


def encode(latents, wt, bit_bias, padded, ahead):
    _, cols, images, width = latents.shape
    bits = wt.shape[0]
    lanes, edge = cols * images, 2 * images
    return pl.pallas_call(
        encode_kernel,
        in_specs=[HBM] * 3,
        out_specs=[VMEM] * 10,
        out_shape=[
            pltpu.VMEM((4, cols, images, width), BF),
            spaced((4, bits, lanes)),
            spaced((4, padded, edge), BF),
            spaced((4, padded, edge), BF),
            spaced((2, padded, lanes), BF),
            spaced((2, padded, lanes), BF),
            spaced((bits, 128)),
            spaced(wt.shape, BF),
            spaced(bit_bias.shape),
            pltpu.VMEM((ahead, cols, images, width), BF),
        ],
        scratch_shapes=[pltpu.SemaphoreType.DMA((6 + ahead,))],
        compiler_params=params(8),
        cost_estimate=cost(2 * 4 * lanes * width * 256, 4 * lanes * width * 2),
        name="encode",
    )(latents, wt, bit_bias)


def outward_row(x, w, squash, total):
    x = x.reshape(-1, x.shape[-1])
    code = (2.0 * squash - 1.0).astype(BF)
    return dot(w, x, ((1,), (1,))), total + dot(code, x, ((1,), (0,)))


def middle_kernel(
    x_hbm, c_hbm, wt_ref, bias_ref, up_w_ref, sqe_ref, mass_in, xa_ref,
    x_ref, sq_ref, ea_ref, eb_ref, mass_ref, cg_ref, up_ref,
    c_ref, sem,
):
    rows, (inside, bits, lanes), early = x_hbm.shape[0], sq_ref.shape, cg_ref.shape[0]
    edge = 2 * x_hbm.shape[2]
    ahead = xa_ref.shape[0]
    copies = [pltpu.make_async_copy(x_hbm.at[2 + k], x_ref.at[k - ahead], sem.at[k]) for k in range(ahead, inside)]
    outward = [pltpu.make_async_copy(c_hbm.at[k], c_ref.at[k], sem.at[inside + k]) for k in range(early)]
    for copy in copies + outward:
        copy.start()
    wt, bias = wt_ref[...], to_column(bias_ref[...], bits)
    wa_even = even("wa")
    mass = mass_in[...]
    for k in range(inside):
        if k >= ahead:
            copies[k - ahead].wait()
        logits = logits_of(split_row(xa_ref, x_ref, k, ahead), wt, bias)
        squash = jax.nn.sigmoid(logits)
        sq_ref[k] = squash
        mass = add_mass(mass, squash)
        put_edges(ea_ref, eb_ref, k, logits, edge, wa_even)
    row = to_row(jnp.sum(mass, axis=1, keepdims=True), bits)
    mass_ref[...] = jnp.concatenate([row, jnp.zeros((1, 128 - bits), F32)], axis=1)
    total = jnp.zeros(up_ref.shape, F32)
    for k, copy in enumerate(outward):
        copy.wait()
        cg_ref[k], total = outward_row(c_ref[k], up_w_ref[...], row_of(sqe_ref, sq_ref, k, rows), total)
    up_ref[...] = total


def middle(latents, cotangent, wt, bias, w_up, squash, mass, x_ahead, padded, early):
    rows, cols, images, width = latents.shape
    bits, lanes, edge = wt.shape[0], cols * images, 2 * images
    inside = rows - 4
    return pl.pallas_call(
        middle_kernel,
        in_specs=[HBM] * 2 + [VMEM] * 6,
        out_specs=[VMEM] * 7,
        out_shape=[
            pltpu.VMEM((inside - x_ahead.shape[0], cols, images, width), BF),
            spaced((inside, bits, lanes)),
            spaced((inside, padded, edge), BF),
            spaced((inside, padded, edge), BF),
            spaced((1, 128)),
            spaced((early, bits, lanes)),
            spaced((bits, width)),
        ],
        scratch_shapes=[pltpu.VMEM((early, cols, images, width), BF), pltpu.SemaphoreType.DMA((inside + early,))],
        compiler_params=params(12),
        cost_estimate=cost(2 * (inside + 2 * early) * lanes * width * 256, (inside + early) * lanes * width * 2),
        name="middle",
    )(latents, cotangent, wt, bias, w_up, squash, mass, x_ahead)


def pack_kernel(ea_e, eb_e, ea_m, eb_m, ha_a, ha_b, mass_ref, ea_ref, eb_ref):
    rows, _, edge = ea_ref.shape
    rows -= 5
    lanes = ha_a.shape[2]
    spare = 8
    wa_even, ha_even = even("wa"), even("ha")
    for out, outer, inner in ((ea_ref, ea_e, ea_m), (eb_ref, eb_e, eb_m)):
        for k in range(2):
            out[2 + k] = outer[k]
            out[rows + k] = outer[2 + k]
        for k in range(rows - 4):
            out[4 + k] = inner[k]
    for k in range(2):
        for at, side in ((k, jnp.where(ha_even, ha_b[k], ha_a[k])), (rows + 2 + k, jnp.where(ha_even, ha_a[k], ha_b[k]))):
            left, right = side[:, :edge], side[:, lanes - edge :]
            ea_ref[at] = jnp.where(wa_even, right, left)
            eb_ref[at] = jnp.where(wa_even, left, right)
    row = mass_ref[...]
    high = row.astype(BF).astype(F32)
    middle = (row - high).astype(BF).astype(F32)
    parts = jnp.concatenate([high, middle, row - high - middle, jnp.zeros((spare - 3, edge), F32)], axis=0).astype(BF)
    ea_ref[rows + 4, :spare] = parts
    eb_ref[rows + 4, :spare] = parts


def pack(edges, halos, mass, rows):
    _, padded, edge = edges[0].shape
    return pl.pallas_call(
        pack_kernel,
        in_specs=[VMEM] * 7,
        out_specs=[VMEM] * 2,
        out_shape=[spaced((rows + 5, padded, edge), BF)] * 2,
        compiler_params=params(2),
        cost_estimate=cost(0, 2**18),
        name="pack",
    )(*edges, *halos, mass)


def window(t, cell):
    wide = t.shape[1] - 2 * cell
    return (t[:, :wide] + t[:, cell : cell + wide] + t[:, 2 * cell :]) / 9.0


def slope_of(t, cell):
    pooled = window(t, cell)
    lp, lq = jnp.log(pooled), jnp.log(1.0 - pooled)
    return local_weight * (lq - lp), jnp.sum(pooled * (lq - lp) - lq, axis=0, keepdims=True)


def gradients(t, cell, squash, cg, stacked):
    bits, lanes = squash.shape
    half = stacked.shape[0] // 2
    steep = squash * (1.0 - squash)
    g = 2.0 * cg + 0.98 * window(t, cell)
    stacked[:bits] = (g * steep).astype(BF)
    stacked[half : half + bits] = steep.astype(BF)
    values = stacked[...]
    columns = values[:, :128].astype(F32)
    for k in range(1, lanes // 128):
        columns += values[:, k * 128 : (k + 1) * 128].astype(F32)
    return g, values, columns


def inner_kernel(
    c_hbm, xe_ref, xa_ref, xm_ref, sqe_ref, sqm_ref, ha_a, ha_b, cg_in, up_in, up_w_ref, after,
    cg_ref, up_ref, g_ref, slope_ref, ent_ref, acc_ref, columns_ref, pe_ref,
    c_ref, stacked, sem,
):
    late, bits, lanes = cg_ref.shape
    early, rows = cg_in.shape[0], g_ref.shape[0]
    images, width = xe_ref.shape[2:]
    edge = 2 * images
    copies = [pltpu.make_async_copy(c_hbm.at[early + k], c_ref.at[k], sem.at[k]) for k in range(late)]
    for copy in copies:
        copy.start()
    ha_even = even("ha")
    stacked[...] = jnp.zeros_like(stacked)
    for k in range(2):
        a, b = ha_a[k, :bits], ha_b[k, :bits]
        pe_ref[k] = prob_of(jax.nn.sigmoid(jnp.where(ha_even, b, a).astype(F32)))
        pe_ref[rows + 2 + k] = prob_of(jax.nn.sigmoid(jnp.where(ha_even, a, b).astype(F32)))
    for r in range(rows):
        pe_ref[2 + r] = prob_of(row_of(sqe_ref, sqm_ref, r, rows))
    def slope_row(e):
        slope_ref[e], entropy = slope_of(pe_ref[e] + pe_ref[e + 1] + pe_ref[e + 2], images)
        if 1 <= e <= rows:
            ent_ref[e - 1 : e] = entropy

    slope_row(0)
    slope_row(1)
    total = up_in[...]
    acc = jnp.zeros(acc_ref.shape, F32)
    columns = jnp.zeros(columns_ref.shape, F32)
    for r in range(rows):
        squash = row_of(sqe_ref, sqm_ref, r, rows)
        if r < early:
            cg = cg_in[r]
        else:
            copies[r - early].wait()
            cg, total = outward_row(c_ref[r - early], up_w_ref[...], squash, total)
            cg_ref[r - early] = cg
        slope_row(r + 2)
        t = slope_ref[r] + slope_ref[r + 1] + slope_ref[r + 2]
        g_ref[r], values, sums = gradients(t, images, squash[:, edge : lanes - edge], cg[:, edge : lanes - edge], stacked.at[r % 2])
        x = latent_row(xe_ref, xa_ref, xm_ref, r, rows)[2:-2].reshape(lanes - 2 * edge, width)
        acc += dot(values, x, ((1,), (0,)))
        columns += sums
    acc_ref[...] = acc
    columns_ref[...] = columns
    up_ref[...] = total


def inner(cotangent, x_edge, x_ahead, x_middle, sq_edge, sq_middle, ha_a, ha_b, cg, up, w_up, after):
    rows, cols, images, width = cotangent.shape
    early, bits, lanes = cg.shape
    late, edge = rows - early, 2 * images
    padded = -(-bits // 16) * 16
    return pl.pallas_call(
        inner_kernel,
        in_specs=[HBM] + [VMEM] * 10 + [pl.BlockSpec(memory_space=pl.ANY)],
        out_specs=[VMEM] * 8,
        out_shape=[
            spaced((late, bits, lanes)),
            spaced((bits, width)),
            spaced((rows, bits, lanes - 2 * edge)),
            spaced((rows + 2, bits, lanes - edge)),
            spaced((rows, lanes - edge)),
            spaced((2 * padded, width)),
            spaced((2 * padded, 128)),
            spaced((rows + 4, bits, lanes)),
        ],
        scratch_shapes=[
            pltpu.VMEM((late, cols, images, width), BF),
            pltpu.VMEM((2, 2 * padded, lanes - 2 * edge), BF),
            pltpu.SemaphoreType.DMA((late,)),
        ],
        compiler_params=params(12),
        cost_estimate=cost(2 * (2 * late + rows) * lanes * width * 256, late * lanes * width * 2),
        name="inner",
    )(cotangent, x_edge, x_ahead, x_middle, sq_edge, sq_middle, ha_a, ha_b, cg, up, w_up, after)


def outer_kernel(
    xe_ref, xa_ref, xm_ref, sqe_ref, sqm_ref, cg0_ref, cg1_ref, wa_a, wa_b, slope_ref, pe_ref, acc_in, columns_in, up_ref, mass_ref,
    g_ref, ent_ref, mine_ref, other_ref,
    near, stacked,
):
    rows, bits, _ = g_ref.shape
    images, width = xe_ref.shape[2:]
    lanes, edge = sqe_ref.shape[2], 2 * images
    half = stacked.shape[1] // 2
    wa_even, ha_even = even("wa"), even("ha")
    stacked[...] = jnp.zeros_like(stacked)
    ends = lambda v: jnp.concatenate([v[:, :edge], v[:, lanes - edge :]], axis=1)
    probs = []
    for e in range(rows + 4):
        a, b = wa_a[e, :bits], wa_b[e, :bits]
        left = prob_of(jax.nn.sigmoid(jnp.where(wa_even, b, a).astype(F32)))
        right = prob_of(jax.nn.sigmoid(jnp.where(wa_even, a, b).astype(F32)))
        own = pe_ref[e]
        probs.append((jnp.concatenate([left, own[:, :edge]], axis=1), jnp.concatenate([own[:, lanes - edge :], right], axis=1)))
    for e in range(rows + 2):
        sides = [probs[e][i] + probs[e + 1][i] + probs[e + 2][i] for i in range(2)]
        (left, left_ent), (right, right_ent) = [slope_of(t, images) for t in sides]
        if 1 <= e <= rows:
            ent_ref[e - 1 : e] = jnp.concatenate([left_ent[:, images:], right_ent[:, :images]], axis=1)
        inside = slope_ref[e]
        near[e, 0] = jnp.concatenate([left, inside[:, :edge]], axis=1)
        near[e, 1] = jnp.concatenate([inside[:, lanes - 2 * edge :], right], axis=1)
    acc, columns = acc_in[...], columns_in[...]
    for r in range(rows):
        squash, cg = ends(row_of(sqe_ref, sqm_ref, r, rows)), ends(split_row(cg0_ref, cg1_ref, r, cg0_ref.shape[0]))
        x = latent_row(xe_ref, xa_ref, xm_ref, r, rows)
        x = jnp.concatenate([x[:2].reshape(edge, width), x[-2:].reshape(edge, width)], axis=0)
        spread = jnp.concatenate([window(near[r, i] + near[r + 1, i] + near[r + 2, i], images) for i in range(2)], axis=1)
        steep = squash * (1.0 - squash)
        g = 2.0 * cg + 0.98 * spread
        g_ref[r] = g
        at = stacked.at[r % 2]
        at[:bits] = (g * steep).astype(BF)
        at[half : half + bits] = steep.astype(BF)
        values = at[...]
        acc += dot(values, x, ((1,), (0,)))
        for k in range(2 * edge // 128):
            columns += values[:, k * 128 : (k + 1) * 128].astype(F32)
    total = jnp.sum(columns, axis=1, keepdims=True)
    others = sum(ref[rows + 4, :8].astype(F32)[k : k + 1] for ref in (wa_a, wa_b) for k in range(3))
    rows_of = (to_row(total[:bits], bits), to_row(total[half : half + bits], bits), mass_ref[:, :bits], others[:, :bits])
    low, high = slice(0, width // 2), slice(width // 2, width)
    pieces = ((0, acc[:bits]), (bits, acc[half : half + bits]), (2 * bits, up_ref[...]))
    lead = 3 * bits
    for ref, flip in ((mine_ref, False), (other_ref, True)):
        ref[lead:, :] = jnp.zeros((ref.shape[0] - lead, ref.shape[1]), F32)
        take_low = jnp.logical_xor(ha_even, flip)
        for at, piece in pieces:
            ref[at : at + bits] = jnp.where(take_low, piece[:, low], piece[:, high])
        ref[lead : lead + 1, :bits] = rows_of[0]
        ref[lead : lead + 1, 128 : 128 + bits] = rows_of[1]
        ref[lead + 1 : lead + 2, :bits] = rows_of[2]
        ref[lead + 1 : lead + 2, 128 : 128 + bits] = rows_of[3]


def outer(rows, width, images, *operands):
    bits = operands[3].shape[1]
    padded = -(-bits // 16) * 16
    sums = -(-(3 * bits + 2) // 8) * 8
    edge = 2 * images
    return pl.pallas_call(
        outer_kernel,
        in_specs=[VMEM] * len(operands),
        out_specs=[VMEM] * 4,
        out_shape=[spaced((rows, bits, 2 * edge)), spaced((rows, edge)), spaced((sums, width // 2)), spaced((sums, width // 2))],
        scratch_shapes=[pltpu.VMEM((rows + 2, 2, bits, 2 * edge), F32), pltpu.VMEM((2, 2 * padded, 2 * edge), BF)],
        compiler_params=params(8),
        cost_estimate=cost(2 * rows * 2 * edge * width * 256, 2**20),
        name="outer",
    )(*operands)


def back_kernel(count, first, slots, with_entropy, gi_ref, go_ref, sqe_ref, sqm_ref, wt_ref, *refs):
    sums, refs = refs[: len(slots)], refs[len(slots) :]
    rows, bits, edge = go_ref.shape
    edge //= 2
    extra = []
    if with_entropy:
        ei_ref, eo_ref, out_hbm, ent_hbm, out_ref, sem, ent_ref, ent_sem = refs
        images = ent_ref.shape[2]
        for c in range(ent_ref.shape[1]):
            at = (c - 1) * images
            last = c == ent_ref.shape[1] - 1
            ent_ref[:, c, :] = ei_ref[:, at : at + images] if c > 0 and not last else eo_ref[:, images:] if last else eo_ref[:, :images]
        extra = [pltpu.make_async_copy(ent_ref, ent_hbm, ent_sem)]
        extra[0].start()
    else:
        _, out_hbm, out_ref, sem = refs
    at = 3 * bits + 1
    marginal = sum(ref[at : at + 1, lane : lane + bits] for ref, lane in zip(sums, slots)) / count
    drift = to_column(0.98 * margin_weight * jnp.log((1.0 - marginal) / marginal), bits)
    wt = wt_ref[...]
    copies = [pltpu.make_async_copy(out_ref.at[k], out_hbm.at[first + k], sem.at[k]) for k in range(out_ref.shape[0])]
    for k, copy in enumerate(copies):
        r = first + k
        squash = row_of(sqe_ref, sqm_ref, r, rows)
        g = jnp.concatenate([go_ref[r][:, :edge], gi_ref[r], go_ref[r][:, edge:]], axis=1)
        grad = ((g - drift) * (squash * (1.0 - squash))).astype(BF)
        out_ref[k] = dot(grad, wt, ((0,), (0,))).astype(BF).reshape(out_ref.shape[1:])
        copy.start()
    for copy in copies + extra:
        copy.wait()


def back(shape, g_inner, g_outer, sq_edge, sq_middle, wt, marginal, count, first, rows, entropies=(), onto=()):
    arrays, slots = zip(*marginal)
    operands = [g_inner, g_outer, sq_edge, sq_middle, wt, *arrays, *entropies]
    outs, scratch = [spaced(shape, BF)], [pltpu.VMEM((rows, *shape[1:]), BF), pltpu.SemaphoreType.DMA((rows,))]
    if entropies:
        outs.append(spaced(shape[:3]))
        scratch += [pltpu.VMEM(shape[:3], F32), pltpu.SemaphoreType.DMA]
    cells = rows * shape[1] * shape[2] * shape[3]
    return pl.pallas_call(
        functools.partial(back_kernel, count, first, slots, bool(entropies)),
        in_specs=[VMEM] * len(operands) + [HBM] * len(onto),
        out_specs=[HBM] * len(outs),
        out_shape=outs,
        input_output_aliases={len(operands): 0} if onto else {},
        scratch_shapes=scratch,
        compiler_params=params(16),
        cost_estimate=cost(2 * cells * 256, cells * 2),
        name="back",
    )(*operands, *onto)


def finish_kernel(count, mine_ref, other_ref, marginal_ref, down_ref, bias_ref, up_ref):
    bits = marginal_ref.shape[1]
    core = even("ha")
    a, b = mine_ref[...], other_ref[...]
    sums = jnp.concatenate([jnp.where(core, a, b), jnp.where(core, b, a)], axis=1)
    mass = mine_ref[3 * bits + 1 : 3 * bits + 2, :bits]
    marginal = mass / count
    marginal_ref[...] = marginal
    drift_row = margin_weight * jnp.log((1.0 - marginal) / marginal)
    drift = to_column(drift_row, bits)
    down = (sums[:bits] - 0.98 * drift * sums[bits : 2 * bits]) / count
    down_ref[...] = down
    bias_ref[...] = (mine_ref[3 * bits : 3 * bits + 1, :bits] - 0.98 * drift_row * mine_ref[3 * bits : 3 * bits + 1, 128 : 128 + bits]) / count
    up_ref[...] = sums[2 * bits : 3 * bits] / count


def finish(mine, other, bits, count):
    width = 2 * mine.shape[1]
    return pl.pallas_call(
        functools.partial(finish_kernel, count),
        out_shape=[
            jax.ShapeDtypeStruct((1, bits), F32),
            jax.ShapeDtypeStruct((bits, width), F32),
            jax.ShapeDtypeStruct((1, bits), F32),
            jax.ShapeDtypeStruct((bits, width), F32),
        ],
        compiler_params=pltpu.CompilerParams(vmem_limit_bytes=8 * 2**20),
        name="finish",
    )(mine, other)


def swap(x, axis, mask):
    return lax.ppermute(x, axis, [(i, i ^ mask) for i in range(lax.axis_size(axis))])


def swap_outer(x, axis):
    count = lax.axis_size(axis)
    return lax.ppermute(x, axis, [(i, (((i + 1) ^ 1) - 1) % count) for i in range(count)])


def exchanged(x, axis, stride, radix):
    return [swap(x, axis, d * stride) for d in ((3, 1, 2) if radix == 4 else (1,))]


def stages(count, stride):
    while stride < count:
        radix = 4 if stride * 4 <= count else 2
        yield stride, radix
        stride *= radix


def summed(x, axis, start):
    for stride, radix in stages(lax.axis_size(axis), start):
        x = sum(exchanged(x, axis, stride, radix), x)
    return x


def local(latents, cotangent, w_down, bit_bias, w_up):
    rows, cols, images, width = latents.shape
    bits = w_down.shape[1]
    columns = lax.axis_size("wa")
    count = rows * cols * images * lax.axis_size("ha") * columns
    padded = -(-bits // 8) * 8
    early, first = EARLY_ROWS, FIRST_ROWS
    near = lambda a: pltpu.with_memory_space_constraint(a, pltpu.HBM)
    resident = lambda a: pltpu.with_memory_space_constraint(a, pltpu.VMEM)
    latents, cotangent = near(latents), near(cotangent)
    x_e, sq_e, ea_e, eb_e, ra, rb, mass, wt, bias, x_a = encode(latents, near(w_down.T), near(bit_bias.reshape(1, bits)), padded, AHEAD_ROWS)
    ha_b, ha_a = swap_outer(rb, "ha"), swap(ra, "ha", 1)
    x_m, sq_m, ea_m, eb_m, mass, cg0, up = middle(latents, cotangent, wt, bias, w_up, sq_e, mass, resident(x_a), padded, early)
    x_e, x_a, x_m = resident(x_e), resident(x_a), resident(x_m)
    ea, eb = pack((ea_e, eb_e, ea_m, eb_m), (ha_a, ha_b), mass, rows)
    wa_a, wa_b = swap(ea, "wa", 1), swap_outer(eb, "wa")
    cg1, up, g_inner, slope, ent_inner, acc, sums, probs = inner(cotangent, x_e, x_a, x_m, sq_e, sq_m, ha_a, ha_b, cg0, up, w_up, ea)
    g_outer, ent_outer, mine, other = outer(
        rows, width, images, x_e, x_a, x_m, sq_e, sq_m, cg0, cg1, wa_a, wa_b, slope, probs, acc, sums, up, mass
    )
    sums = mine + swap(other, "ha", 1)
    sums = summed(sums, "ha", 2)
    run = functools.partial(back, latents.shape, g_inner, g_outer, sq_e, sq_m, wt)
    if columns == 4:
        opposite, *rest = [swap(sums, "wa", d) for d in (2, 1, 3)]
        known = [(sums, 0), (sums, 128), (opposite, 0)]
        grad_latents, entropy = run(known, count, 0, first, entropies=(ent_inner, ent_outer))
        near_sums, grad_latents = lax.optimization_barrier((sums + opposite, grad_latents))
        sums = sum(rest, near_sums)
    else:
        sums = summed(sums, "wa", 1)
        grad_latents, entropy = run([(sums, 0)], count, 0, first, entropies=(ent_inner, ent_outer))
    partner = swap(sums, "ha", 1)
    (grad_latents,) = run([(sums, 0)], count, first, rows - first, onto=(grad_latents,))
    marginal, grad_down, grad_bias, grad_up = finish(sums, partner, bits, count)
    return grad_latents, entropy, marginal.reshape(bits), grad_down.T, grad_bias.reshape(bits), grad_up


def solution(mesh):
    placed = (P("ha", "wa", None, None), P("ha", "wa", None, None), P(), P(), P())
    return jax.shard_map(
        local,
        mesh=mesh,
        in_specs=placed,
        out_specs=(P("ha", "wa", None, None), P("ha", "wa", None), P(), P(), P(), P()),
        check_vma=False,
    )
```

```python
import functools
import math

import jax
import jax.numpy as jnp
from jax import lax
from jax.experimental import pallas as pl
from jax.experimental.pallas import tpu as pltpu
from jax.sharding import PartitionSpec as P


local_weight = 4.0
margin_weight = 4.0
BF, F32 = jnp.bfloat16, jnp.float32
EARLY_ROWS, FIRST_ROWS, AHEAD_ROWS = 4, 6, 2


VMEM = pl.BlockSpec(memory_space=pltpu.VMEM)
HBM = pl.BlockSpec(memory_space=pltpu.HBM)


def params(mib):
    return pltpu.CompilerParams(vmem_limit_bytes=mib * 2**20)


def cost(flops, bytes_accessed):
    return pl.CostEstimate(flops=flops, bytes_accessed=bytes_accessed, transcendentals=0)


def dot(a, b, dims):
    return lax.dot_general(a, b, (dims, ((), ())), preferred_element_type=F32)


def to_column(row, n):
    eye = lax.broadcasted_iota(jnp.int32, (n, n), 0) == lax.broadcasted_iota(jnp.int32, (n, n), 1)
    return jnp.sum(jnp.where(eye, row, 0.0), axis=1, keepdims=True)


def to_row(column, n):
    eye = lax.broadcasted_iota(jnp.int32, (n, n), 0) == lax.broadcasted_iota(jnp.int32, (n, n), 1)
    return jnp.sum(jnp.where(eye, column, 0.0), axis=0, keepdims=True)


def even(axis):
    return lax.rem(lax.axis_index(axis), 2) == 0


def prob_of(squash):
    return 0.01 + 0.98 * squash


def spaced(shape, dtype=F32):
    return jax.ShapeDtypeStruct(shape, dtype)


def border(r, rows):
    return r if r < 2 else r - (rows - 4) if r >= rows - 2 else None


def latent_row(edge_ref, ahead_ref, middle_ref, r, rows):
    k = border(r, rows)
    return edge_ref[k] if k is not None else split_row(ahead_ref, middle_ref, r - 2, ahead_ref.shape[0])


def row_of(edge_ref, middle_ref, r, rows):
    k = border(r, rows)
    return middle_ref[r - 2] if k is None else edge_ref[k]


def split_row(edge_ref, middle_ref, r, count):
    return edge_ref[r] if r < count else middle_ref[r - count]


def logits_of(x, wt, bias):
    return dot(wt, x.reshape(-1, x.shape[-1]), ((1,), (1,))) + bias


def add_mass(mass, squash):
    prob = prob_of(squash)
    for k in range(prob.shape[1] // 128):
        mass += prob[:, k * 128 : (k + 1) * 128]
    return mass


def put_edges(ea_ref, eb_ref, k, logits, edge, wa_even):
    bits, lanes = logits.shape
    left, right = logits[:, :edge].astype(BF), logits[:, lanes - edge :].astype(BF)
    ea_ref[k, :bits] = jnp.where(wa_even, right, left)
    eb_ref[k, :bits] = jnp.where(wa_even, left, right)


def encode_kernel(x_hbm, wt_hbm, bias_hbm, x_ref, sq_ref, ea_ref, eb_ref, ra_ref, rb_ref, mass_ref, wt_ref, bias_ref, ahead_ref, sem):
    rows, bits = x_hbm.shape[0], sq_ref.shape[1]
    edge = 2 * x_hbm.shape[2]
    order = (0, 1, rows - 2, rows - 1, *range(2, 2 + ahead_ref.shape[0]))
    small = [pltpu.make_async_copy(wt_hbm, wt_ref, sem.at[4]), pltpu.make_async_copy(bias_hbm, bias_ref, sem.at[5])]
    place = lambda k: x_ref.at[k] if k < 4 else ahead_ref.at[k - 4]
    copies = [pltpu.make_async_copy(x_hbm.at[r], place(k), sem.at[k if k < 4 else k + 2]) for k, r in enumerate(order)]
    copies, ahead = copies[:4], copies[4:]
    for copy in small + copies + ahead:
        copy.start()
    for copy in small:
        copy.wait()
    wt, bias = wt_ref[...], to_column(bias_ref[...], bits)
    wa_even, ha_even = even("wa"), even("ha")
    mass = jnp.zeros((bits, 128), F32)
    packed = []
    for k, copy in enumerate(copies):
        copy.wait()
        logits = logits_of(x_ref[k], wt, bias)
        squash = jax.nn.sigmoid(logits)
        sq_ref[k] = squash
        mass = add_mass(mass, squash)
        put_edges(ea_ref, eb_ref, k, logits, edge, wa_even)
        packed.append(logits.astype(BF))
        if k >= 2:
            ra_ref[k - 2, :bits] = jnp.where(ha_even, packed[k], packed[k - 2])
            rb_ref[k - 2, :bits] = jnp.where(ha_even, packed[k - 2], packed[k])
    mass_ref[...] = mass
    for copy in ahead:
        copy.wait()


def encode(latents, wt, bit_bias, padded, ahead):
    _, cols, images, width = latents.shape
    bits = wt.shape[0]
    lanes, edge = cols * images, 2 * images
    return pl.pallas_call(
        encode_kernel,
        in_specs=[HBM] * 3,
        out_specs=[VMEM] * 10,
        out_shape=[
            pltpu.VMEM((4, cols, images, width), BF),
            spaced((4, bits, lanes)),
            spaced((4, padded, edge), BF),
            spaced((4, padded, edge), BF),
            spaced((2, padded, lanes), BF),
            spaced((2, padded, lanes), BF),
            spaced((bits, 128)),
            spaced(wt.shape, BF),
            spaced(bit_bias.shape),
            pltpu.VMEM((ahead, cols, images, width), BF),
        ],
        scratch_shapes=[pltpu.SemaphoreType.DMA((6 + ahead,))],
        compiler_params=params(8),
        cost_estimate=cost(2 * 4 * lanes * width * 256, 4 * lanes * width * 2),
        name="encode",
    )(latents, wt, bit_bias)


def outward_row(x, w, squash, total):
    x = x.reshape(-1, x.shape[-1])
    code = (2.0 * squash - 1.0).astype(BF)
    return dot(w, x, ((1,), (1,))), total + dot(code, x, ((1,), (0,)))


def middle_kernel(
    x_hbm, c_hbm, wt_ref, bias_ref, up_w_ref, sqe_ref, mass_in, xa_ref,
    x_ref, sq_ref, ea_ref, eb_ref, mass_ref, cg_ref, up_ref,
    c_ref, sem,
):
    rows, (inside, bits, lanes), early = x_hbm.shape[0], sq_ref.shape, cg_ref.shape[0]
    edge = 2 * x_hbm.shape[2]
    ahead = xa_ref.shape[0]
    copies = [pltpu.make_async_copy(x_hbm.at[2 + k], x_ref.at[k - ahead], sem.at[k]) for k in range(ahead, inside)]
    outward = [pltpu.make_async_copy(c_hbm.at[k], c_ref.at[k], sem.at[inside + k]) for k in range(early)]
    for copy in copies + outward:
        copy.start()
    wt, bias = wt_ref[...], to_column(bias_ref[...], bits)
    wa_even = even("wa")
    mass = mass_in[...]
    for k in range(inside):
        if k >= ahead:
            copies[k - ahead].wait()
        logits = logits_of(split_row(xa_ref, x_ref, k, ahead), wt, bias)
        squash = jax.nn.sigmoid(logits)
        sq_ref[k] = squash
        mass = add_mass(mass, squash)
        put_edges(ea_ref, eb_ref, k, logits, edge, wa_even)
    row = to_row(jnp.sum(mass, axis=1, keepdims=True), bits)
    mass_ref[...] = jnp.concatenate([row, jnp.zeros((1, 128 - bits), F32)], axis=1)
    total = jnp.zeros(up_ref.shape, F32)
    for k, copy in enumerate(outward):
        copy.wait()
        cg_ref[k], total = outward_row(c_ref[k], up_w_ref[...], row_of(sqe_ref, sq_ref, k, rows), total)
    up_ref[...] = total


def middle(latents, cotangent, wt, bias, w_up, squash, mass, x_ahead, padded, early):
    rows, cols, images, width = latents.shape
    bits, lanes, edge = wt.shape[0], cols * images, 2 * images
    inside = rows - 4
    return pl.pallas_call(
        middle_kernel,
        in_specs=[HBM] * 2 + [VMEM] * 6,
        out_specs=[VMEM] * 7,
        out_shape=[
            pltpu.VMEM((inside - x_ahead.shape[0], cols, images, width), BF),
            spaced((inside, bits, lanes)),
            spaced((inside, padded, edge), BF),
            spaced((inside, padded, edge), BF),
            spaced((1, 128)),
            spaced((early, bits, lanes)),
            spaced((bits, width)),
        ],
        scratch_shapes=[pltpu.VMEM((early, cols, images, width), BF), pltpu.SemaphoreType.DMA((inside + early,))],
        compiler_params=params(12),
        cost_estimate=cost(2 * (inside + 2 * early) * lanes * width * 256, (inside + early) * lanes * width * 2),
        name="middle",
    )(latents, cotangent, wt, bias, w_up, squash, mass, x_ahead)


def heights(bits, count):
    main = bits // 8 * 8
    return main, count * main, -(-count * (bits - main) // 8) * 8


def unpack(ref, k, bits, count):
    main, at, spare = heights(bits, count)
    body = ref[k * main : (k + 1) * main].astype(F32)
    if not spare:
        return body
    left = bits - main
    return jnp.concatenate([body, ref[at : at + spare].astype(F32)[k * left : (k + 1) * left]], axis=0)


def pack_kernel(bits, ea_e, eb_e, ea_m, eb_m, ha_a, ha_b, mass_ref, ea_ref, eb_ref):
    rows, edge = ea_e.shape[0] + ea_m.shape[0], ea_ref.shape[1]
    lanes = ha_a.shape[2]
    main, at, spare = heights(bits, rows + 4)
    wa_even, ha_even = even("wa"), even("ha")
    above, below = [], []
    for k in range(2):
        above.append(jnp.where(ha_even, ha_b[k], ha_a[k]))
        below.append(jnp.where(ha_even, ha_a[k], ha_b[k]))
    row = mass_ref[...]
    high = row.astype(BF).astype(F32)
    middle = (row - high).astype(BF).astype(F32)
    parts = jnp.concatenate([high, middle, row - high - middle, jnp.zeros((5, edge), F32)], axis=0)
    for out, outer, inner, take_right in ((ea_ref, ea_e, ea_m, wa_even), (eb_ref, eb_e, eb_m, jnp.logical_not(wa_even))):
        pick = lambda side: jnp.where(take_right, side[:, lanes - edge :], side[:, :edge])
        values = [*map(pick, above), outer[0], outer[1], *[inner[k] for k in range(rows - 4)], outer[2], outer[3], *map(pick, below)]
        for e, value in enumerate(values):
            out[e * main : (e + 1) * main] = value[:main]
        if spare:
            unused = spare - (bits - main) * len(values)
            left = [value.astype(F32)[main:bits] for value in values] + [jnp.zeros((unused, edge), F32)] * (unused > 0)
            out[at : at + spare] = jnp.concatenate(left, axis=0).astype(BF)
        out[at + spare :] = parts.astype(BF)


def pack(edges, halos, mass, rows, bits):
    edge = edges[0].shape[2]
    _, at, spare = heights(bits, rows + 4)
    return pl.pallas_call(
        functools.partial(pack_kernel, bits),
        in_specs=[VMEM] * 7,
        out_specs=[VMEM] * 2,
        out_shape=[spaced((at + spare + 8, edge), BF)] * 2,
        compiler_params=params(2),
        cost_estimate=cost(0, 2**18),
        name="pack",
    )(*edges, *halos, mass)


def window(t, cell):
    wide = t.shape[1] - 2 * cell
    return (t[:, :wide] + t[:, cell : cell + wide] + t[:, 2 * cell :]) / 9.0


def slope_of(t, cell):
    pooled = window(t, cell)
    lp, lq = jnp.log(pooled), jnp.log(1.0 - pooled)
    return local_weight * (lq - lp), jnp.sum(pooled * (lq - lp) - lq, axis=0, keepdims=True)


def gradients(t, cell, squash, cg, stacked):
    bits, lanes = squash.shape
    half = stacked.shape[0] // 2
    steep = squash * (1.0 - squash)
    g = 2.0 * cg + 0.98 * window(t, cell)
    stacked[:bits] = (g * steep).astype(BF)
    stacked[half : half + bits] = steep.astype(BF)
    values = stacked[...]
    columns = values[:, :128].astype(F32)
    for k in range(1, lanes // 128):
        columns += values[:, k * 128 : (k + 1) * 128].astype(F32)
    return g, values, columns


def inner_kernel(
    c_hbm, xe_ref, xa_ref, xm_ref, sqe_ref, sqm_ref, ha_a, ha_b, cg_in, up_in, up_w_ref, after,
    cg_ref, up_ref, g_ref, slope_ref, ent_ref, acc_ref, columns_ref, pe_ref,
    c_ref, stacked, sem,
):
    late, bits, lanes = cg_ref.shape
    early, rows = cg_in.shape[0], g_ref.shape[0]
    images, width = xe_ref.shape[2:]
    edge = 2 * images
    copies = [pltpu.make_async_copy(c_hbm.at[early + k], c_ref.at[k], sem.at[k]) for k in range(late)]
    for copy in copies:
        copy.start()
    ha_even = even("ha")
    stacked[...] = jnp.zeros_like(stacked)
    for k in range(2):
        a, b = ha_a[k, :bits], ha_b[k, :bits]
        pe_ref[k] = prob_of(jax.nn.sigmoid(jnp.where(ha_even, b, a).astype(F32)))
        pe_ref[rows + 2 + k] = prob_of(jax.nn.sigmoid(jnp.where(ha_even, a, b).astype(F32)))
    for r in range(rows):
        pe_ref[2 + r] = prob_of(row_of(sqe_ref, sqm_ref, r, rows))
    def slope_row(e):
        slope_ref[e], entropy = slope_of(pe_ref[e] + pe_ref[e + 1] + pe_ref[e + 2], images)
        if 1 <= e <= rows:
            ent_ref[e - 1 : e] = entropy

    slope_row(0)
    slope_row(1)
    total = up_in[...]
    acc = jnp.zeros(acc_ref.shape, F32)
    columns = jnp.zeros(columns_ref.shape, F32)
    for r in range(rows):
        squash = row_of(sqe_ref, sqm_ref, r, rows)
        if r < early:
            cg = cg_in[r]
        else:
            copies[r - early].wait()
            cg, total = outward_row(c_ref[r - early], up_w_ref[...], squash, total)
            cg_ref[r - early] = cg
        slope_row(r + 2)
        t = slope_ref[r] + slope_ref[r + 1] + slope_ref[r + 2]
        g_ref[r], values, sums = gradients(t, images, squash[:, edge : lanes - edge], cg[:, edge : lanes - edge], stacked.at[r % 2])
        x = latent_row(xe_ref, xa_ref, xm_ref, r, rows)[2:-2].reshape(lanes - 2 * edge, width)
        acc += dot(values, x, ((1,), (0,)))
        columns += sums
    acc_ref[...] = acc
    columns_ref[...] = columns
    up_ref[...] = total


def inner(cotangent, x_edge, x_ahead, x_middle, sq_edge, sq_middle, ha_a, ha_b, cg, up, w_up, after):
    rows, cols, images, width = cotangent.shape
    early, bits, lanes = cg.shape
    late, edge = rows - early, 2 * images
    padded = -(-bits // 16) * 16
    return pl.pallas_call(
        inner_kernel,
        in_specs=[HBM] + [VMEM] * 10 + [pl.BlockSpec(memory_space=pl.ANY)],
        out_specs=[VMEM] * 8,
        out_shape=[
            spaced((late, bits, lanes)),
            spaced((bits, width)),
            spaced((rows, bits, lanes - 2 * edge)),
            spaced((rows + 2, bits, lanes - edge)),
            spaced((rows, lanes - edge)),
            spaced((2 * padded, width)),
            spaced((2 * padded, 128)),
            spaced((rows + 4, bits, lanes)),
        ],
        scratch_shapes=[
            pltpu.VMEM((late, cols, images, width), BF),
            pltpu.VMEM((2, 2 * padded, lanes - 2 * edge), BF),
            pltpu.SemaphoreType.DMA((late,)),
        ],
        compiler_params=params(12),
        cost_estimate=cost(2 * (2 * late + rows) * lanes * width * 256, late * lanes * width * 2),
        name="inner",
    )(cotangent, x_edge, x_ahead, x_middle, sq_edge, sq_middle, ha_a, ha_b, cg, up, w_up, after)


def outer_kernel(
    xe_ref, xa_ref, xm_ref, sqe_ref, sqm_ref, cg0_ref, cg1_ref, wa_a, wa_b, slope_ref, pe_ref, acc_in, columns_in, up_ref, mass_ref,
    g_ref, ent_ref, mine_ref, other_ref,
    near, stacked,
):
    rows, bits, _ = g_ref.shape
    images, width = xe_ref.shape[2:]
    lanes, edge = sqe_ref.shape[2], 2 * images
    half = stacked.shape[1] // 2
    wa_even, ha_even = even("wa"), even("ha")
    stacked[...] = jnp.zeros_like(stacked)
    ends = lambda v: jnp.concatenate([v[:, :edge], v[:, lanes - edge :]], axis=1)
    probs = []
    for e in range(rows + 4):
        a, b = unpack(wa_a, e, bits, rows + 4), unpack(wa_b, e, bits, rows + 4)
        left = prob_of(jax.nn.sigmoid(jnp.where(wa_even, b, a)))
        right = prob_of(jax.nn.sigmoid(jnp.where(wa_even, a, b)))
        own = pe_ref[e]
        probs.append((jnp.concatenate([left, own[:, :edge]], axis=1), jnp.concatenate([own[:, lanes - edge :], right], axis=1)))
    for e in range(rows + 2):
        sides = [probs[e][i] + probs[e + 1][i] + probs[e + 2][i] for i in range(2)]
        (left, left_ent), (right, right_ent) = [slope_of(t, images) for t in sides]
        if 1 <= e <= rows:
            ent_ref[e - 1 : e] = jnp.concatenate([left_ent[:, images:], right_ent[:, :images]], axis=1)
        inside = slope_ref[e]
        near[e, 0] = jnp.concatenate([left, inside[:, :edge]], axis=1)
        near[e, 1] = jnp.concatenate([inside[:, lanes - 2 * edge :], right], axis=1)
    acc, columns = acc_in[...], columns_in[...]
    for r in range(rows):
        squash, cg = ends(row_of(sqe_ref, sqm_ref, r, rows)), ends(split_row(cg0_ref, cg1_ref, r, cg0_ref.shape[0]))
        x = latent_row(xe_ref, xa_ref, xm_ref, r, rows)
        x = jnp.concatenate([x[:2].reshape(edge, width), x[-2:].reshape(edge, width)], axis=0)
        spread = jnp.concatenate([window(near[r, i] + near[r + 1, i] + near[r + 2, i], images) for i in range(2)], axis=1)
        steep = squash * (1.0 - squash)
        g = 2.0 * cg + 0.98 * spread
        g_ref[r] = g
        at = stacked.at[r % 2]
        at[:bits] = (g * steep).astype(BF)
        at[half : half + bits] = steep.astype(BF)
        values = at[...]
        acc += dot(values, x, ((1,), (0,)))
        for k in range(2 * edge // 128):
            columns += values[:, k * 128 : (k + 1) * 128].astype(F32)
    total = jnp.sum(columns, axis=1, keepdims=True)
    others = sum(ref[ref.shape[0] - 8 :].astype(F32)[k : k + 1] for ref in (wa_a, wa_b) for k in range(3))
    rows_of = (to_row(total[:bits], bits), to_row(total[half : half + bits], bits), mass_ref[:, :bits], others[:, :bits])
    low, high = slice(0, width // 2), slice(width // 2, width)
    pieces = ((0, acc[:bits]), (bits, acc[half : half + bits]), (2 * bits, up_ref[...]))
    lead = 3 * bits
    for ref, flip in ((mine_ref, False), (other_ref, True)):
        ref[lead:, :] = jnp.zeros((ref.shape[0] - lead, ref.shape[1]), F32)
        take_low = jnp.logical_xor(ha_even, flip)
        for at, piece in pieces:
            ref[at : at + bits] = jnp.where(take_low, piece[:, low], piece[:, high])
        ref[lead : lead + 1, :bits] = rows_of[0]
        ref[lead : lead + 1, 128 : 128 + bits] = rows_of[1]
        ref[lead + 1 : lead + 2, :bits] = rows_of[2]
        ref[lead + 1 : lead + 2, 128 : 128 + bits] = rows_of[3]


def outer(rows, width, images, *operands):
    bits = operands[3].shape[1]
    padded = -(-bits // 16) * 16
    sums = -(-(3 * bits + 2) // 8) * 8
    edge = 2 * images
    return pl.pallas_call(
        outer_kernel,
        in_specs=[VMEM] * len(operands),
        out_specs=[VMEM] * 4,
        out_shape=[spaced((rows, bits, 2 * edge)), spaced((rows, edge)), spaced((sums, width // 2)), spaced((sums, width // 2))],
        scratch_shapes=[pltpu.VMEM((rows + 2, 2, bits, 2 * edge), F32), pltpu.VMEM((2, 2 * padded, 2 * edge), BF)],
        compiler_params=params(8),
        cost_estimate=cost(2 * rows * 2 * edge * width * 256, 2**20),
        name="outer",
    )(*operands)


def back_kernel(count, slots, gi_ref, go_ref, sqe_ref, sqm_ref, wt_ref, *refs):
    sums = refs[: len(slots)]
    ei_ref, eo_ref, out_hbm, ent_hbm, rest_ref, out_ref, sem, ent_ref, ent_sem = refs[len(slots) :]
    rows, bits, edge = go_ref.shape
    edge //= 2
    cols, images = ent_ref.shape[1:]
    for c in range(cols):
        at = (c - 1) * images
        ent_ref[:, c, :] = eo_ref[:, :images] if c == 0 else eo_ref[:, images:] if c == cols - 1 else ei_ref[:, at : at + images]
    entropy_copy = pltpu.make_async_copy(ent_ref, ent_hbm, ent_sem)
    entropy_copy.start()
    at = 3 * bits + 1
    marginal = sum(ref[at : at + 1, lane : lane + bits] for ref, lane in zip(sums, slots)) / count
    drift = to_column(0.98 * margin_weight * jnp.log((1.0 - marginal) / marginal), bits)
    wt = wt_ref[...]
    first = out_ref.shape[0]
    copies = [pltpu.make_async_copy(out_ref.at[r], out_hbm.at[r], sem.at[r]) for r in range(first)]
    for r in range(rows):
        squash = row_of(sqe_ref, sqm_ref, r, rows)
        g = jnp.concatenate([go_ref[r][:, :edge], gi_ref[r], go_ref[r][:, edge:]], axis=1)
        grad = ((g - drift) * (squash * (1.0 - squash))).astype(BF)
        value = dot(grad, wt, ((0,), (0,))).astype(BF).reshape(out_ref.shape[1:])
        if r < first:
            out_ref[r] = value
            copies[r].start()
        else:
            rest_ref[r - first] = value
    for copy in copies + [entropy_copy]:
        copy.wait()


def back(shape, g_inner, g_outer, sq_edge, sq_middle, wt, marginal, count, first, ent_inner, ent_outer):
    arrays, slots = zip(*marginal)
    operands = [g_inner, g_outer, sq_edge, sq_middle, wt, *arrays, ent_inner, ent_outer]
    cells = math.prod(shape)
    return pl.pallas_call(
        functools.partial(back_kernel, count, slots),
        in_specs=[VMEM] * len(operands),
        out_specs=[HBM, HBM, VMEM],
        out_shape=[spaced(shape, BF), spaced(shape[:3]), pltpu.VMEM((shape[0] - first, *shape[1:]), BF)],
        scratch_shapes=[
            pltpu.VMEM((first, *shape[1:]), BF),
            pltpu.SemaphoreType.DMA((first,)),
            pltpu.VMEM(shape[:3], F32),
            pltpu.SemaphoreType.DMA,
        ],
        compiler_params=params(16),
        cost_estimate=cost(2 * cells * 256, cells * 2),
        name="back",
    )(*operands)


def store_kernel(rest_ref, _, out_hbm, sem):
    count = rest_ref.shape[0]
    first = out_hbm.shape[0] - count
    copies = [pltpu.make_async_copy(rest_ref.at[k], out_hbm.at[first + k], sem.at[k]) for k in range(count)]
    for copy in copies:
        copy.start()
    for copy in copies:
        copy.wait()


def store(rest, onto):
    return pl.pallas_call(
        store_kernel,
        in_specs=[VMEM, HBM],
        out_specs=HBM,
        out_shape=spaced(onto.shape, BF),
        input_output_aliases={1: 0},
        scratch_shapes=[pltpu.SemaphoreType.DMA((rest.shape[0],))],
        compiler_params=params(2),
        cost_estimate=cost(0, rest.size * 2),
        name="store",
    )(rest, onto)


def finish_kernel(count, mine_ref, other_ref, marginal_ref, down_ref, bias_ref, up_ref):
    bits = marginal_ref.shape[1]
    core = even("ha")
    a, b = mine_ref[...], other_ref[...]
    sums = jnp.concatenate([jnp.where(core, a, b), jnp.where(core, b, a)], axis=1)
    mass = mine_ref[3 * bits + 1 : 3 * bits + 2, :bits]
    marginal = mass / count
    marginal_ref[...] = marginal
    drift_row = margin_weight * jnp.log((1.0 - marginal) / marginal)
    drift = to_column(drift_row, bits)
    down = (sums[:bits] - 0.98 * drift * sums[bits : 2 * bits]) / count
    down_ref[...] = down
    bias_ref[...] = (mine_ref[3 * bits : 3 * bits + 1, :bits] - 0.98 * drift_row * mine_ref[3 * bits : 3 * bits + 1, 128 : 128 + bits]) / count
    up_ref[...] = sums[2 * bits : 3 * bits] / count


def finish(mine, other, bits, count):
    width = 2 * mine.shape[1]
    return pl.pallas_call(
        functools.partial(finish_kernel, count),
        out_shape=[
            jax.ShapeDtypeStruct((1, bits), F32),
            jax.ShapeDtypeStruct((bits, width), F32),
            jax.ShapeDtypeStruct((1, bits), F32),
            jax.ShapeDtypeStruct((bits, width), F32),
        ],
        compiler_params=pltpu.CompilerParams(vmem_limit_bytes=8 * 2**20),
        name="finish",
    )(mine, other)


def swap(x, axis, mask):
    return lax.ppermute(x, axis, [(i, i ^ mask) for i in range(lax.axis_size(axis))])


def swap_outer(x, axis):
    count = lax.axis_size(axis)
    return lax.ppermute(x, axis, [(i, (((i + 1) ^ 1) - 1) % count) for i in range(count)])


def exchanged(x, axis, stride, radix):
    return [swap(x, axis, d * stride) for d in ((3, 1, 2) if radix == 4 else (1,))]


def stages(count, stride):
    while stride < count:
        radix = 4 if stride * 4 <= count else 2
        yield stride, radix
        stride *= radix


def summed(x, axis, start):
    for stride, radix in stages(lax.axis_size(axis), start):
        x = sum(exchanged(x, axis, stride, radix), x)
    return x


def local(latents, cotangent, w_down, bit_bias, w_up):
    rows, cols, images, width = latents.shape
    bits = w_down.shape[1]
    columns = lax.axis_size("wa")
    count = rows * cols * images * lax.axis_size("ha") * columns
    padded = -(-bits // 8) * 8
    early, first = EARLY_ROWS, FIRST_ROWS
    near = lambda a: pltpu.with_memory_space_constraint(a, pltpu.HBM)
    resident = lambda a: pltpu.with_memory_space_constraint(a, pltpu.VMEM)
    latents, cotangent = near(latents), near(cotangent)
    x_e, sq_e, ea_e, eb_e, ra, rb, mass, wt, bias, x_a = encode(latents, near(w_down.T), near(bit_bias.reshape(1, bits)), padded, AHEAD_ROWS)
    ha_b = swap_outer(rb, "ha")
    ha_a = swap(ra, "ha", 1)
    x_m, sq_m, ea_m, eb_m, mass, cg0, up = middle(latents, cotangent, wt, bias, w_up, sq_e, mass, resident(x_a), padded, early)
    x_e, x_a, x_m = resident(x_e), resident(x_a), resident(x_m)
    ea, eb = pack((ea_e, eb_e, ea_m, eb_m), (ha_a, ha_b), mass, rows, bits)
    wa_a, wa_b = swap(ea, "wa", 1), swap_outer(eb, "wa")
    cg1, up, g_inner, slope, ent_inner, acc, sums, probs = inner(cotangent, x_e, x_a, x_m, sq_e, sq_m, ha_a, ha_b, cg0, up, w_up, ea)
    g_outer, ent_outer, mine, other = outer(
        rows, width, images, x_e, x_a, x_m, sq_e, sq_m, cg0, cg1, wa_a, wa_b, slope, probs, acc, sums, up, mass
    )
    sums = mine + swap(other, "ha", 1)
    sums = summed(sums, "ha", 2)
    run = functools.partial(back, latents.shape, g_inner, g_outer, sq_e, sq_m, wt)
    if columns == 4:
        opposite, *rest = [swap(sums, "wa", d) for d in (2, 1, 3)]
        known = [(sums, 0), (sums, 128), (opposite, 0)]
        grad_latents, entropy, rest_rows = run(known, count, first, ent_inner, ent_outer)
        near_sums, grad_latents = lax.optimization_barrier((sums + opposite, grad_latents))
        sums = sum(rest, near_sums)
    else:
        sums = summed(sums, "wa", 1)
        grad_latents, entropy, rest_rows = run([(sums, 0)], count, first, ent_inner, ent_outer)
    partner = swap(sums, "ha", 1)
    grad_latents = store(rest_rows, grad_latents)
    marginal, grad_down, grad_bias, grad_up = finish(sums, partner, bits, count)
    return grad_latents, entropy, marginal.reshape(bits), grad_down.T, grad_bias.reshape(bits), grad_up


def solution(mesh):
    placed = (P("ha", "wa", None, None), P("ha", "wa", None, None), P(), P(), P())
    return jax.shard_map(
        local,
        mesh=mesh,
        in_specs=placed,
        out_specs=(P("ha", "wa", None, None), P("ha", "wa", None), P(), P(), P(), P()),
        check_vma=False,
    )
```

```python
import functools
import math

import jax
import jax.numpy as jnp
from jax import lax
from jax.experimental import pallas as pl
from jax.experimental.pallas import tpu as pltpu
from jax.sharding import PartitionSpec as P


local_weight = 4.0
margin_weight = 4.0
BF, F32 = jnp.bfloat16, jnp.float32
EARLY_ROWS, FIRST_ROWS, AHEAD_ROWS = 4, 6, 2


VMEM = pl.BlockSpec(memory_space=pltpu.VMEM)
HBM = pl.BlockSpec(memory_space=pltpu.HBM)


def params(mib):
    return pltpu.CompilerParams(vmem_limit_bytes=mib * 2**20)


def cost(flops, bytes_accessed):
    return pl.CostEstimate(flops=flops, bytes_accessed=bytes_accessed, transcendentals=0)


def dot(a, b, dims):
    return lax.dot_general(a, b, (dims, ((), ())), preferred_element_type=F32)


def to_column(row, n):
    eye = lax.broadcasted_iota(jnp.int32, (n, n), 0) == lax.broadcasted_iota(jnp.int32, (n, n), 1)
    return jnp.sum(jnp.where(eye, row, 0.0), axis=1, keepdims=True)


def to_row(column, n):
    eye = lax.broadcasted_iota(jnp.int32, (n, n), 0) == lax.broadcasted_iota(jnp.int32, (n, n), 1)
    return jnp.sum(jnp.where(eye, column, 0.0), axis=0, keepdims=True)


def even(axis):
    return lax.rem(lax.axis_index(axis), 2) == 0


def prob_of(squash):
    return 0.01 + 0.98 * squash


def spaced(shape, dtype=F32):
    return jax.ShapeDtypeStruct(shape, dtype)


def border(r, rows):
    return r if r < 2 else r - (rows - 4) if r >= rows - 2 else None


def latent_row(edge_ref, ahead_ref, middle_ref, r, rows):
    k = border(r, rows)
    return edge_ref[k] if k is not None else split_row(ahead_ref, middle_ref, r - 2, ahead_ref.shape[0])


def row_of(edge_ref, middle_ref, r, rows):
    k = border(r, rows)
    return middle_ref[r - 2] if k is None else edge_ref[k]


def split_row(edge_ref, middle_ref, r, count):
    return edge_ref[r] if r < count else middle_ref[r - count]


def logits_of(x, wt, bias):
    return dot(wt, x.reshape(-1, x.shape[-1]), ((1,), (1,))) + bias


def add_mass(mass, squash):
    prob = prob_of(squash)
    for k in range(prob.shape[1] // 128):
        mass += prob[:, k * 128 : (k + 1) * 128]
    return mass


def put_edges(ea_ref, eb_ref, k, logits, edge, wa_even):
    bits, lanes = logits.shape
    left, right = logits[:, :edge].astype(BF), logits[:, lanes - edge :].astype(BF)
    ea_ref[k, :bits] = jnp.where(wa_even, right, left)
    eb_ref[k, :bits] = jnp.where(wa_even, left, right)


def encode_kernel(x_hbm, wt_hbm, bias_hbm, x_ref, sq_ref, ea_ref, eb_ref, ra_ref, rb_ref, mass_ref, wt_ref, bias_ref, ahead_ref, sem):
    rows, bits = x_hbm.shape[0], sq_ref.shape[1]
    edge = 2 * x_hbm.shape[2]
    order = (0, 1, rows - 2, rows - 1, *range(2, 2 + ahead_ref.shape[0]))
    small = [pltpu.make_async_copy(wt_hbm, wt_ref, sem.at[4]), pltpu.make_async_copy(bias_hbm, bias_ref, sem.at[5])]
    place = lambda k: x_ref.at[k] if k < 4 else ahead_ref.at[k - 4]
    copies = [pltpu.make_async_copy(x_hbm.at[r], place(k), sem.at[k if k < 4 else k + 2]) for k, r in enumerate(order)]
    copies, ahead = copies[:4], copies[4:]
    for copy in small + copies + ahead:
        copy.start()
    for copy in small:
        copy.wait()
    wt, bias = wt_ref[...], to_column(bias_ref[...], bits)
    wa_even, ha_even = even("wa"), even("ha")
    mass = jnp.zeros((bits, 128), F32)
    packed = []
    for k, copy in enumerate(copies):
        copy.wait()
        logits = logits_of(x_ref[k], wt, bias)
        squash = jax.nn.sigmoid(logits)
        sq_ref[k] = squash
        mass = add_mass(mass, squash)
        put_edges(ea_ref, eb_ref, k, logits, edge, wa_even)
        packed.append(logits.astype(BF))
        if k >= 2:
            ra_ref[k - 2, :bits] = jnp.where(ha_even, packed[k], packed[k - 2])
            rb_ref[k - 2, :bits] = jnp.where(ha_even, packed[k - 2], packed[k])
    mass_ref[...] = mass
    for copy in ahead:
        copy.wait()


def encode(latents, wt, bit_bias, padded, ahead):
    _, cols, images, width = latents.shape
    bits = wt.shape[0]
    lanes, edge = cols * images, 2 * images
    return pl.pallas_call(
        encode_kernel,
        in_specs=[HBM] * 3,
        out_specs=[VMEM] * 10,
        out_shape=[
            pltpu.VMEM((4, cols, images, width), BF),
            spaced((4, bits, lanes)),
            spaced((4, padded, edge), BF),
            spaced((4, padded, edge), BF),
            spaced((2, padded, lanes), BF),
            spaced((2, padded, lanes), BF),
            spaced((bits, 128)),
            spaced(wt.shape, BF),
            spaced(bit_bias.shape),
            pltpu.VMEM((ahead, cols, images, width), BF),
        ],
        scratch_shapes=[pltpu.SemaphoreType.DMA((6 + ahead,))],
        compiler_params=params(8),
        cost_estimate=cost(2 * 4 * lanes * width * 256, 4 * lanes * width * 2),
        name="encode",
    )(latents, wt, bit_bias)


def outward_row(x, w, squash, total):
    x = x.reshape(-1, x.shape[-1])
    code = (2.0 * squash - 1.0).astype(BF)
    return dot(w, x, ((1,), (1,))), total + dot(code, x, ((1,), (0,)))


def middle_kernel(
    x_hbm, c_hbm, wt_ref, bias_ref, up_w_ref, sqe_ref, mass_in, xa_ref,
    x_ref, sq_ref, ea_ref, eb_ref, mass_ref, cg_ref, up_ref,
    c_ref, sem,
):
    rows, (inside, bits, lanes), early = x_hbm.shape[0], sq_ref.shape, cg_ref.shape[0]
    edge = 2 * x_hbm.shape[2]
    ahead = xa_ref.shape[0]
    copies = [pltpu.make_async_copy(x_hbm.at[2 + k], x_ref.at[k - ahead], sem.at[k]) for k in range(ahead, inside)]
    outward = [pltpu.make_async_copy(c_hbm.at[k], c_ref.at[k], sem.at[inside + k]) for k in range(early)]
    for copy in copies + outward:
        copy.start()
    wt, bias = wt_ref[...], to_column(bias_ref[...], bits)
    wa_even = even("wa")
    mass = mass_in[...]
    for k in range(inside):
        if k >= ahead:
            copies[k - ahead].wait()
        logits = logits_of(split_row(xa_ref, x_ref, k, ahead), wt, bias)
        squash = jax.nn.sigmoid(logits)
        sq_ref[k] = squash
        mass = add_mass(mass, squash)
        put_edges(ea_ref, eb_ref, k, logits, edge, wa_even)
    row = to_row(jnp.sum(mass, axis=1, keepdims=True), bits)
    mass_ref[...] = jnp.concatenate([row, jnp.zeros((1, 128 - bits), F32)], axis=1)
    total = jnp.zeros(up_ref.shape, F32)
    for k, copy in enumerate(outward):
        copy.wait()
        cg_ref[k], total = outward_row(c_ref[k], up_w_ref[...], row_of(sqe_ref, sq_ref, k, rows), total)
    up_ref[...] = total


def middle(latents, cotangent, wt, bias, w_up, squash, mass, x_ahead, padded, early):
    rows, cols, images, width = latents.shape
    bits, lanes, edge = wt.shape[0], cols * images, 2 * images
    inside = rows - 4
    return pl.pallas_call(
        middle_kernel,
        in_specs=[HBM] * 2 + [VMEM] * 6,
        out_specs=[VMEM] * 7,
        out_shape=[
            pltpu.VMEM((inside - x_ahead.shape[0], cols, images, width), BF),
            spaced((inside, bits, lanes)),
            spaced((inside, padded, edge), BF),
            spaced((inside, padded, edge), BF),
            spaced((1, 128)),
            spaced((early, bits, lanes)),
            spaced((bits, width)),
        ],
        scratch_shapes=[pltpu.VMEM((early, cols, images, width), BF), pltpu.SemaphoreType.DMA((inside + early,))],
        compiler_params=params(12),
        cost_estimate=cost(2 * (inside + 2 * early) * lanes * width * 256, (inside + early) * lanes * width * 2),
        name="middle",
    )(latents, cotangent, wt, bias, w_up, squash, mass, x_ahead)


def heights(bits, count):
    main = bits // 8 * 8
    return main, count * main, -(-count * (bits - main) // 8) * 8


def unpack(ref, k, bits, count):
    main, at, spare = heights(bits, count)
    body = ref[k * main : (k + 1) * main].astype(F32)
    if not spare:
        return body
    left = bits - main
    return jnp.concatenate([body, ref[at : at + spare].astype(F32)[k * left : (k + 1) * left]], axis=0)


def pack_kernel(bits, ea_e, eb_e, ea_m, eb_m, ha_a, ha_b, mass_ref, ea_ref, eb_ref):
    rows, edge = ea_e.shape[0] + ea_m.shape[0], ea_ref.shape[1]
    lanes = ha_a.shape[2]
    main, at, spare = heights(bits, rows + 4)
    wa_even, ha_even = even("wa"), even("ha")
    above, below = [], []
    for k in range(2):
        above.append(jnp.where(ha_even, ha_b[k], ha_a[k]))
        below.append(jnp.where(ha_even, ha_a[k], ha_b[k]))
    row = mass_ref[...]
    high = row.astype(BF).astype(F32)
    middle = (row - high).astype(BF).astype(F32)
    parts = jnp.concatenate([high, middle, row - high - middle, jnp.zeros((5, edge), F32)], axis=0)
    for out, outer, inner, take_right in ((ea_ref, ea_e, ea_m, wa_even), (eb_ref, eb_e, eb_m, jnp.logical_not(wa_even))):
        pick = lambda side: jnp.where(take_right, side[:, lanes - edge :], side[:, :edge])
        values = [*map(pick, above), outer[0], outer[1], *[inner[k] for k in range(rows - 4)], outer[2], outer[3], *map(pick, below)]
        for e, value in enumerate(values):
            out[e * main : (e + 1) * main] = value[:main]
        if spare:
            unused = spare - (bits - main) * len(values)
            left = [value.astype(F32)[main:bits] for value in values] + [jnp.zeros((unused, edge), F32)] * (unused > 0)
            out[at : at + spare] = jnp.concatenate(left, axis=0).astype(BF)
        out[at + spare :] = parts.astype(BF)


def pack(edges, halos, mass, rows, bits):
    edge = edges[0].shape[2]
    _, at, spare = heights(bits, rows + 4)
    return pl.pallas_call(
        functools.partial(pack_kernel, bits),
        in_specs=[VMEM] * 7,
        out_specs=[VMEM] * 2,
        out_shape=[spaced((at + spare + 8, edge), BF)] * 2,
        compiler_params=params(2),
        cost_estimate=cost(0, 2**18),
        name="pack",
    )(*edges, *halos, mass)


def window(t, cell):
    wide = t.shape[1] - 2 * cell
    return (t[:, :wide] + t[:, cell : cell + wide] + t[:, 2 * cell :]) / 9.0


def slope_of(t, cell):
    pooled = window(t, cell)
    lp, lq = jnp.log(pooled), jnp.log(1.0 - pooled)
    return local_weight * (lq - lp), jnp.sum(pooled * (lq - lp) - lq, axis=0, keepdims=True)


def gradients(t, cell, squash, cg, stacked):
    bits, lanes = squash.shape
    half = stacked.shape[0] // 2
    steep = squash * (1.0 - squash)
    g = 2.0 * cg + 0.98 * window(t, cell)
    stacked[:bits] = (g * steep).astype(BF)
    stacked[half : half + bits] = steep.astype(BF)
    values = stacked[...]
    columns = values[:, :128].astype(F32)
    for k in range(1, lanes // 128):
        columns += values[:, k * 128 : (k + 1) * 128].astype(F32)
    return g, values, columns


def inner_kernel(
    c_ref, xe_ref, xa_ref, xm_ref, sqe_ref, sqm_ref, ha_a, ha_b, cg_in, up_in, up_w_ref, after,
    cg_ref, up_ref, g_ref, slope_ref, ent_ref, acc_ref, columns_ref, pe_ref,
    stacked,
):
    _, bits, lanes = cg_ref.shape
    early, rows = cg_in.shape[0], g_ref.shape[0]
    images, width = xe_ref.shape[2:]
    edge = 2 * images
    ha_even = even("ha")
    stacked[...] = jnp.zeros_like(stacked)
    for k in range(2):
        a, b = ha_a[k, :bits], ha_b[k, :bits]
        pe_ref[k] = prob_of(jax.nn.sigmoid(jnp.where(ha_even, b, a).astype(F32)))
        pe_ref[rows + 2 + k] = prob_of(jax.nn.sigmoid(jnp.where(ha_even, a, b).astype(F32)))
    for r in range(rows):
        pe_ref[2 + r] = prob_of(row_of(sqe_ref, sqm_ref, r, rows))
    def slope_row(e):
        slope_ref[e], entropy = slope_of(pe_ref[e] + pe_ref[e + 1] + pe_ref[e + 2], images)
        if 1 <= e <= rows:
            ent_ref[e - 1 : e] = entropy

    slope_row(0)
    slope_row(1)
    total = up_in[...]
    acc = jnp.zeros(acc_ref.shape, F32)
    columns = jnp.zeros(columns_ref.shape, F32)
    for r in range(rows):
        squash = row_of(sqe_ref, sqm_ref, r, rows)
        if r < early:
            cg = cg_in[r]
        else:
            cg, total = outward_row(c_ref[r], up_w_ref[...], squash, total)
            cg_ref[r - early] = cg
        slope_row(r + 2)
        t = slope_ref[r] + slope_ref[r + 1] + slope_ref[r + 2]
        g_ref[r], values, sums = gradients(t, images, squash[:, edge : lanes - edge], cg[:, edge : lanes - edge], stacked.at[r % 2])
        x = latent_row(xe_ref, xa_ref, xm_ref, r, rows)[2:-2].reshape(lanes - 2 * edge, width)
        acc += dot(values, x, ((1,), (0,)))
        columns += sums
    acc_ref[...] = acc
    columns_ref[...] = columns
    up_ref[...] = total


def inner(cotangent, x_edge, x_ahead, x_middle, sq_edge, sq_middle, ha_a, ha_b, cg, up, w_up, after):
    rows, _, images, width = cotangent.shape
    early, bits, lanes = cg.shape
    late, edge = rows - early, 2 * images
    padded = -(-bits // 16) * 16
    return pl.pallas_call(
        inner_kernel,
        in_specs=[VMEM] * 11 + [pl.BlockSpec(memory_space=pl.ANY)],
        out_specs=[VMEM] * 8,
        out_shape=[
            spaced((late, bits, lanes)),
            spaced((bits, width)),
            spaced((rows, bits, lanes - 2 * edge)),
            spaced((rows + 2, bits, lanes - edge)),
            spaced((rows, lanes - edge)),
            spaced((2 * padded, width)),
            spaced((2 * padded, 128)),
            spaced((rows + 4, bits, lanes)),
        ],
        scratch_shapes=[
            pltpu.VMEM((2, 2 * padded, lanes - 2 * edge), BF),
        ],
        compiler_params=params(12),
        cost_estimate=cost(2 * (2 * late + rows) * lanes * width * 256, late * lanes * width * 2),
        name="inner",
    )(cotangent, x_edge, x_ahead, x_middle, sq_edge, sq_middle, ha_a, ha_b, cg, up, w_up, after)


def outer_kernel(
    xe_ref, xa_ref, xm_ref, sqe_ref, sqm_ref, cg0_ref, cg1_ref, wa_a, wa_b, slope_ref, pe_ref, acc_in, columns_in, up_ref, mass_ref,
    g_ref, ent_ref, mine_ref, other_ref,
    near, stacked,
):
    rows, bits, _ = g_ref.shape
    images, width = xe_ref.shape[2:]
    lanes, edge = sqe_ref.shape[2], 2 * images
    half = stacked.shape[1] // 2
    wa_even, ha_even = even("wa"), even("ha")
    stacked[...] = jnp.zeros_like(stacked)
    ends = lambda v: jnp.concatenate([v[:, :edge], v[:, lanes - edge :]], axis=1)
    probs = []
    for e in range(rows + 4):
        a, b = unpack(wa_a, e, bits, rows + 4), unpack(wa_b, e, bits, rows + 4)
        left = prob_of(jax.nn.sigmoid(jnp.where(wa_even, b, a)))
        right = prob_of(jax.nn.sigmoid(jnp.where(wa_even, a, b)))
        own = pe_ref[e]
        probs.append((jnp.concatenate([left, own[:, :edge]], axis=1), jnp.concatenate([own[:, lanes - edge :], right], axis=1)))
    for e in range(rows + 2):
        sides = [probs[e][i] + probs[e + 1][i] + probs[e + 2][i] for i in range(2)]
        (left, left_ent), (right, right_ent) = [slope_of(t, images) for t in sides]
        if 1 <= e <= rows:
            ent_ref[e - 1 : e] = jnp.concatenate([left_ent[:, images:], right_ent[:, :images]], axis=1)
        inside = slope_ref[e]
        near[e, 0] = jnp.concatenate([left, inside[:, :edge]], axis=1)
        near[e, 1] = jnp.concatenate([inside[:, lanes - 2 * edge :], right], axis=1)
    acc, columns = acc_in[...], columns_in[...]
    for r in range(rows):
        squash, cg = ends(row_of(sqe_ref, sqm_ref, r, rows)), ends(split_row(cg0_ref, cg1_ref, r, cg0_ref.shape[0]))
        x = latent_row(xe_ref, xa_ref, xm_ref, r, rows)
        x = jnp.concatenate([x[:2].reshape(edge, width), x[-2:].reshape(edge, width)], axis=0)
        spread = jnp.concatenate([window(near[r, i] + near[r + 1, i] + near[r + 2, i], images) for i in range(2)], axis=1)
        steep = squash * (1.0 - squash)
        g = 2.0 * cg + 0.98 * spread
        g_ref[r] = g
        at = stacked.at[r % 2]
        at[:bits] = (g * steep).astype(BF)
        at[half : half + bits] = steep.astype(BF)
        values = at[...]
        acc += dot(values, x, ((1,), (0,)))
        for k in range(2 * edge // 128):
            columns += values[:, k * 128 : (k + 1) * 128].astype(F32)
    total = jnp.sum(columns, axis=1, keepdims=True)
    others = sum(ref[ref.shape[0] - 8 :].astype(F32)[k : k + 1] for ref in (wa_a, wa_b) for k in range(3))
    rows_of = (to_row(total[:bits], bits), to_row(total[half : half + bits], bits), mass_ref[:, :bits], others[:, :bits])
    low, high = slice(0, width // 2), slice(width // 2, width)
    pieces = ((0, acc[:bits]), (bits, acc[half : half + bits]), (2 * bits, up_ref[...]))
    lead = 3 * bits
    for ref, flip in ((mine_ref, False), (other_ref, True)):
        ref[lead:, :] = jnp.zeros((ref.shape[0] - lead, ref.shape[1]), F32)
        take_low = jnp.logical_xor(ha_even, flip)
        for at, piece in pieces:
            ref[at : at + bits] = jnp.where(take_low, piece[:, low], piece[:, high])
        ref[lead : lead + 1, :bits] = rows_of[0]
        ref[lead : lead + 1, 128 : 128 + bits] = rows_of[1]
        ref[lead + 1 : lead + 2, :bits] = rows_of[2]
        ref[lead + 1 : lead + 2, 128 : 128 + bits] = rows_of[3]


def outer(rows, width, images, *operands):
    bits = operands[3].shape[1]
    padded = -(-bits // 16) * 16
    sums = -(-(3 * bits + 2) // 8) * 8
    edge = 2 * images
    return pl.pallas_call(
        outer_kernel,
        in_specs=[VMEM] * len(operands),
        out_specs=[VMEM] * 4,
        out_shape=[spaced((rows, bits, 2 * edge)), spaced((rows, edge)), spaced((sums, width // 2)), spaced((sums, width // 2))],
        scratch_shapes=[pltpu.VMEM((rows + 2, 2, bits, 2 * edge), F32), pltpu.VMEM((2, 2 * padded, 2 * edge), BF)],
        compiler_params=params(8),
        cost_estimate=cost(2 * rows * 2 * edge * width * 256, 2**20),
        name="outer",
    )(*operands)


def back_kernel(count, slots, gi_ref, go_ref, sqe_ref, sqm_ref, wt_ref, *refs):
    sums = refs[: len(slots)]
    ei_ref, eo_ref, out_hbm, ent_hbm, rest_ref, out_ref, sem, ent_ref, ent_sem = refs[len(slots) :]
    rows, bits, edge = go_ref.shape
    edge //= 2
    cols, images = ent_ref.shape[1:]
    for c in range(cols):
        at = (c - 1) * images
        ent_ref[:, c, :] = eo_ref[:, :images] if c == 0 else eo_ref[:, images:] if c == cols - 1 else ei_ref[:, at : at + images]
    entropy_copy = pltpu.make_async_copy(ent_ref, ent_hbm, ent_sem)
    entropy_copy.start()
    at = 3 * bits + 1
    marginal = sum(ref[at : at + 1, lane : lane + bits] for ref, lane in zip(sums, slots)) / count
    drift = to_column(0.98 * margin_weight * jnp.log((1.0 - marginal) / marginal), bits)
    wt = wt_ref[...]
    first = out_ref.shape[0]
    copies = [pltpu.make_async_copy(out_ref.at[r], out_hbm.at[r], sem.at[r]) for r in range(first)]
    for r in range(rows):
        squash = row_of(sqe_ref, sqm_ref, r, rows)
        g = jnp.concatenate([go_ref[r][:, :edge], gi_ref[r], go_ref[r][:, edge:]], axis=1)
        grad = ((g - drift) * (squash * (1.0 - squash))).astype(BF)
        value = dot(grad, wt, ((0,), (0,))).astype(BF).reshape(out_ref.shape[1:])
        if r < first:
            out_ref[r] = value
            copies[r].start()
        else:
            rest_ref[r - first] = value
    for copy in copies + [entropy_copy]:
        copy.wait()


def back(shape, g_inner, g_outer, sq_edge, sq_middle, wt, marginal, count, first, ent_inner, ent_outer):
    arrays, slots = zip(*marginal)
    operands = [g_inner, g_outer, sq_edge, sq_middle, wt, *arrays, ent_inner, ent_outer]
    cells = math.prod(shape)
    return pl.pallas_call(
        functools.partial(back_kernel, count, slots),
        in_specs=[VMEM] * len(operands),
        out_specs=[HBM, HBM, VMEM],
        out_shape=[spaced(shape, BF), spaced(shape[:3]), pltpu.VMEM((shape[0] - first, *shape[1:]), BF)],
        scratch_shapes=[
            pltpu.VMEM((first, *shape[1:]), BF),
            pltpu.SemaphoreType.DMA((first,)),
            pltpu.VMEM(shape[:3], F32),
            pltpu.SemaphoreType.DMA,
        ],
        compiler_params=params(16),
        cost_estimate=cost(2 * cells * 256, cells * 2),
        name="back",
    )(*operands)


def store_kernel(rest_ref, _, out_hbm, sem):
    count = rest_ref.shape[0]
    first = out_hbm.shape[0] - count
    copies = [pltpu.make_async_copy(rest_ref.at[k], out_hbm.at[first + k], sem.at[k]) for k in range(count)]
    for copy in copies:
        copy.start()
    for copy in copies:
        copy.wait()


def store(rest, onto):
    return pl.pallas_call(
        store_kernel,
        in_specs=[VMEM, HBM],
        out_specs=HBM,
        out_shape=spaced(onto.shape, BF),
        input_output_aliases={1: 0},
        scratch_shapes=[pltpu.SemaphoreType.DMA((rest.shape[0],))],
        compiler_params=params(2),
        cost_estimate=cost(0, rest.size * 2),
        name="store",
    )(rest, onto)


def finish_kernel(count, mine_ref, other_ref, marginal_ref, down_ref, bias_ref, up_ref):
    bits = marginal_ref.shape[1]
    core = even("ha")
    a, b = mine_ref[...], other_ref[...]
    sums = jnp.concatenate([jnp.where(core, a, b), jnp.where(core, b, a)], axis=1)
    mass = mine_ref[3 * bits + 1 : 3 * bits + 2, :bits]
    marginal = mass / count
    marginal_ref[...] = marginal
    drift_row = margin_weight * jnp.log((1.0 - marginal) / marginal)
    drift = to_column(drift_row, bits)
    down = (sums[:bits] - 0.98 * drift * sums[bits : 2 * bits]) / count
    down_ref[...] = down
    bias_ref[...] = (mine_ref[3 * bits : 3 * bits + 1, :bits] - 0.98 * drift_row * mine_ref[3 * bits : 3 * bits + 1, 128 : 128 + bits]) / count
    up_ref[...] = sums[2 * bits : 3 * bits] / count


def finish(mine, other, bits, count):
    width = 2 * mine.shape[1]
    return pl.pallas_call(
        functools.partial(finish_kernel, count),
        out_shape=[
            jax.ShapeDtypeStruct((1, bits), F32),
            jax.ShapeDtypeStruct((bits, width), F32),
            jax.ShapeDtypeStruct((1, bits), F32),
            jax.ShapeDtypeStruct((bits, width), F32),
        ],
        compiler_params=pltpu.CompilerParams(vmem_limit_bytes=8 * 2**20),
        name="finish",
    )(mine, other)


def swap(x, axis, mask):
    return lax.ppermute(x, axis, [(i, i ^ mask) for i in range(lax.axis_size(axis))])


def swap_outer(x, axis):
    count = lax.axis_size(axis)
    return lax.ppermute(x, axis, [(i, (((i + 1) ^ 1) - 1) % count) for i in range(count)])


def exchanged(x, axis, stride, radix):
    return [swap(x, axis, d * stride) for d in ((3, 1, 2) if radix == 4 else (1,))]


def stages(count, stride):
    while stride < count:
        radix = 4 if stride * 4 <= count else 2
        yield stride, radix
        stride *= radix


def summed(x, axis, start):
    for stride, radix in stages(lax.axis_size(axis), start):
        x = sum(exchanged(x, axis, stride, radix), x)
    return x


def local(latents, cotangent, w_down, bit_bias, w_up):
    rows, cols, images, width = latents.shape
    bits = w_down.shape[1]
    columns = lax.axis_size("wa")
    count = rows * cols * images * lax.axis_size("ha") * columns
    padded = -(-bits // 8) * 8
    early, first = EARLY_ROWS, FIRST_ROWS
    near = lambda a: pltpu.with_memory_space_constraint(a, pltpu.HBM)
    resident = lambda a: pltpu.with_memory_space_constraint(a, pltpu.VMEM)
    held, latents, cotangent = resident(cotangent), near(latents), near(cotangent)
    x_e, sq_e, ea_e, eb_e, ra, rb, mass, wt, bias, x_a = encode(latents, near(w_down.T), near(bit_bias.reshape(1, bits)), padded, AHEAD_ROWS)
    ha_b = swap_outer(rb, "ha")
    ha_a = swap(ra, "ha", 1)
    x_m, sq_m, ea_m, eb_m, mass, cg0, up = middle(latents, cotangent, wt, bias, w_up, sq_e, mass, resident(x_a), padded, early)
    x_e, x_a, x_m = resident(x_e), resident(x_a), resident(x_m)
    ea, eb = pack((ea_e, eb_e, ea_m, eb_m), (ha_a, ha_b), mass, rows, bits)
    wa_a, wa_b = swap(ea, "wa", 1), swap_outer(eb, "wa")
    cg1, up, g_inner, slope, ent_inner, acc, sums, probs = inner(held, x_e, x_a, x_m, sq_e, sq_m, ha_a, ha_b, cg0, up, w_up, ea)
    g_outer, ent_outer, mine, other = outer(
        rows, width, images, x_e, x_a, x_m, sq_e, sq_m, cg0, cg1, wa_a, wa_b, slope, probs, acc, sums, up, mass
    )
    sums = mine + swap(other, "ha", 1)
    sums = summed(sums, "ha", 2)
    run = functools.partial(back, latents.shape, g_inner, g_outer, sq_e, sq_m, wt)
    if columns == 4:
        opposite, *rest = [swap(sums, "wa", d) for d in (2, 1, 3)]
        known = [(sums, 0), (sums, 128), (opposite, 0)]
        grad_latents, entropy, rest_rows = run(known, count, first, ent_inner, ent_outer)
        near_sums, grad_latents = lax.optimization_barrier((sums + opposite, grad_latents))
        sums = sum(rest, near_sums)
    else:
        sums = summed(sums, "wa", 1)
        grad_latents, entropy, rest_rows = run([(sums, 0)], count, first, ent_inner, ent_outer)
    partner = swap(sums, "ha", 1)
    grad_latents = store(rest_rows, grad_latents)
    marginal, grad_down, grad_bias, grad_up = finish(sums, partner, bits, count)
    return grad_latents, entropy, marginal.reshape(bits), grad_down.T, grad_bias.reshape(bits), grad_up


def solution(mesh):
    placed = (P("ha", "wa", None, None), P("ha", "wa", None, None), P(), P(), P())
    return jax.shard_map(
        local,
        mesh=mesh,
        in_specs=placed,
        out_specs=(P("ha", "wa", None, None), P("ha", "wa", None), P(), P(), P(), P()),
        check_vma=False,
    )
```
